512 devices in a mesh: gx: 16 (over z_hi, y, core), gy: 4 (over x), gz: 8 (over z_lo).
Axes of the slice: x: 4, y: 4, z: 16 (z_hi: 2, z_lo: 8; z = z_hi * 8 + z_lo), core: 2. Of those that a mesh axis runs over, the one named last changes fastest.
Arguments:
- body_load: float32 [32, 16, 64, 192], P('gx', 'gy', 'gz'), may hold values from -6 to 6
- probe_load: float32 [32, 16, 64, 192], P('gx', 'gy', 'gz'), may hold values from -6 to 6
- density: float32 [32, 16, 64], P('gx', 'gy', 'gz'), may hold values from 0.3 to 1
- link_types: int32 [32, 16, 64, 7], P('gx', 'gy', 'gz'), may hold values from 0 to 4, as said below
- off_blocks: bfloat16 [4, 192, 192], replicated, may hold values from -0.4375 to 0.4375
- self_blocks: bfloat16 [4, 192, 192], replicated, as said below
- block_owner: int32 [32, 16, 64], P('gx', 'gy', 'gz'), may hold values from 0 to 4095, as said below
Outputs:
- state_field: float32 [32, 16, 64, 192], P('gx', 'gy', 'gz')
- adjoint_field: float32 [32, 16, 64, 192], P('gx', 'gy', 'gz')
- coarse_sensitivity: float32 [4096], P(('gx', 'gy', 'gz'))
The draws below stay inside these ranges and needn't reach their ends.
Inputs may be any that keep to these rules, and one draw needn't show every extreme that they name: `link_types`: entries 0, 1, 2 of a group name the kind of its coupling to the next group along the first, second and third dimension (4: no coupling, always so on the grid's last layer); entry 3 + k equals entry k of the group one step lower along dimension k (4 on the first layer); entry 6 names the kind of the group's own block and is below 4. `block_owner`: every design block is named by exactly 8 node groups. `self_blocks`: each own block is symmetric and its diagonal entries exceed 3.8.
All inputs are finite; a program needn't handle non-finite values.
Results may differ from the reference program's by a relative error of at most 0.0012.
Values may be sent and summed in bfloat16 or wider, within the bound.
A program may use at most 64 MiB of HBM per device.

```python
import math
import jax
import jax.numpy as jnp
from jax import lax

NDOF = 192
NT = 4
NS = 4
ITERS = 4
NX = 32
NY = 16
NZ = 64
BLOCKS = 4096


def draw_density(key, part):
    spread_part = jax.random.uniform(key, (NX, NY, NZ), jnp.float32, 0.6, 1.0)
    position = lax.broadcasted_iota(jnp.float32, (NX, NY, NZ), 0)
    gradient = 0.5 + 0.5 * position / max(NX - 1, 1)
    return spread_part * gradient


def draw_link_types(key, part):
    upper_key = jax.random.fold_in(key, 11)
    own_key = jax.random.fold_in(key, 23)
    upper_types = jax.random.randint(upper_key, (NX, NY, NZ, 3), 0, NT + 1).astype(jnp.int32)
    extents = (NX, NY, NZ)
    uppers = []
    lowers = []
    for k in range(3):
        place = lax.broadcasted_iota(jnp.int32, (NX, NY, NZ), k)
        column = jnp.where(place == extents[k] - 1, NT, upper_types[..., k]).astype(jnp.int32)
        shifted = jnp.roll(column, 1, axis=k)
        lowers.append(jnp.where(place == 0, NT, shifted).astype(jnp.int32))
        uppers.append(column)
    own_types = jax.random.randint(own_key, (NX, NY, NZ), 0, NS).astype(jnp.int32)
    return jnp.stack(uppers + lowers + [own_types], axis=-1).astype(jnp.int32)


def draw_self_blocks(key, part):
    lead_key = jax.random.fold_in(key, 5)
    rest_key = jax.random.fold_in(key, 7)
    limit = math.sqrt(3.0 / NDOF)
    raw_part = jax.random.uniform(rest_key, (NS, NDOF, NDOF), jnp.float32, -limit, limit)
    symmetric = 0.5 * (raw_part + jnp.swapaxes(raw_part, 1, 2))
    leading = jax.random.uniform(lead_key, (NS, NDOF), jnp.float32, 4.0, 8.0)
    rows_index = lax.broadcasted_iota(jnp.int32, (NDOF, NDOF), 0)
    cols_index = lax.broadcasted_iota(jnp.int32, (NDOF, NDOF), 1)
    identity = (rows_index == cols_index).astype(jnp.float32)
    return (symmetric + leading[:, :, None] * identity[None]).astype(jnp.bfloat16)


def draw_block_owner(key, part):
    shuffled = jax.random.permutation(key, NX * NY * NZ).astype(jnp.int32)
    return (shuffled % BLOCKS).reshape(NX, NY, NZ).astype(jnp.int32)


def shard_levels(key, shape, pieces, low, largest):
    gain = 1.0
    for dim, shards_of in pieces:
        heights = jax.random.uniform(jax.random.fold_in(jax.random.fold_in(key, 6), dim), (shards_of,), jnp.float32, low / len(pieces), largest / len(pieces))
        gain = gain * jnp.repeat(jnp.exp(heights), shape[dim] // shards_of).reshape((-1,) + (1,) * (len(shape) - 1 - dim))
    return gain


def centred(key, shape, width, bound, cuts=(), dtype=jnp.bfloat16):
    drawn = width * jax.random.normal(key, shape, jnp.float32)
    if cuts:
        drawn = drawn * shard_levels(key, shape, cuts, -0.22, 0.18)
    return jnp.clip(drawn, -bound, bound).astype(dtype)


def setup_inputs(seed: int = 0) -> dict:
    keys = jax.random.split(jax.random.key(seed), 8)
    return {
        "body_load": centred(keys[0], (NX, NY, NZ, NDOF), 1.0, 6.0, ((0, 16), (1, 4), (2, 8)), jnp.float32),
        "probe_load": centred(keys[1], (NX, NY, NZ, NDOF), 1.0, 6.0, ((0, 16), (1, 4), (2, 8)), jnp.float32),
        "density": draw_density(jax.random.fold_in(keys[7], 71), 0),
        "link_types": draw_link_types(jax.random.fold_in(keys[7], 71), 0),
        "off_blocks": centred(keys[4], (NT, NDOF, NDOF), NDOF ** -0.5, 0.4375),
        "self_blocks": draw_self_blocks(jax.random.fold_in(keys[7], 71), 0),
        "block_owner": draw_block_owner(jax.random.fold_in(keys[7], 71), 0),
    }


def cut_window(padded, shift):
    span_x = padded.shape[1] - 2
    span_y = padded.shape[2] - 2
    span_z = padded.shape[3] - 2
    return padded[:, 1 + shift[0]:1 + shift[0] + span_x, 1 + shift[1]:1 + shift[1] + span_y, 1 + shift[2]:1 + shift[2] + span_z, :]


def masked_product(window, type_codes, blocks, transpose):
    accumulated = jnp.zeros(window.shape, jnp.float32)
    flattened = window.reshape(-1, NDOF)
    for level in range(blocks.shape[0]):
        block = blocks[level]
        if transpose:
            block = block.T
        product = jnp.dot(flattened, block, preferred_element_type=jnp.float32).reshape(window.shape)
        chosen = (type_codes == level)[None, :, :, :, None]
        accumulated = accumulated + jnp.where(chosen, product, 0.0)
    return accumulated


def apply_stiffness(fields_in, stiff_scale, link_types, off_blocks, self_blocks):
    shipped = (fields_in * stiff_scale[None, :, :, :, None]).astype(jnp.bfloat16)
    padded = jnp.pad(shipped, ((0, 0), (1, 1), (1, 1), (1, 1), (0, 0)))
    accumulated = masked_product(cut_window(padded, (0, 0, 0)), link_types[..., 6], self_blocks, False)
    offsets = ((1, 0, 0), (0, 1, 0), (0, 0, 1))
    for k in range(3):
        upper = offsets[k]
        lower = (-upper[0], -upper[1], -upper[2])
        accumulated = accumulated + masked_product(cut_window(padded, upper), link_types[..., k], off_blocks, True)
        accumulated = accumulated + masked_product(cut_window(padded, lower), link_types[..., 3 + k], off_blocks, False)
    return accumulated * stiff_scale[None, :, :, :, None]


def reference(body_load, probe_load, density, link_types, off_blocks, self_blocks, block_owner):
    stiff_scale = density ** 1.5
    diagonals = jnp.diagonal(self_blocks, axis1=1, axis2=2).astype(jnp.float32)
    pivots = diagonals[link_types[..., 6]]
    targets = jnp.stack([body_load, probe_load])
    residual = targets
    solution = jnp.zeros_like(targets)
    for sweep in range(ITERS):
        precond = residual / pivots[None]
        image_field = apply_stiffness(precond, stiff_scale, link_types, off_blocks, self_blocks)
        projected = jnp.sum(residual * image_field, axis=(1, 2, 3, 4))
        energy = jnp.sum(image_field * image_field, axis=(1, 2, 3, 4))
        step_size = projected / (energy + 1e-6)
        solution = solution + step_size[:, None, None, None, None] * precond
        residual = residual - step_size[:, None, None, None, None] * image_field
    applied = targets - residual
    bracket = jnp.sum(solution[1] * applied[0] + solution[0] * applied[1], axis=-1)
    sensitivity = -1.5 * bracket / density
    weighted = density * sensitivity
    owners = block_owner.reshape(-1).astype(jnp.int32)
    numerator = jax.ops.segment_sum(weighted.reshape(-1), owners, num_segments=BLOCKS)
    denominator = jax.ops.segment_sum(density.reshape(-1), owners, num_segments=BLOCKS)
    return solution[0], solution[1], numerator / denominator
```

```python
import functools

import jax
import jax.numpy as jnp
from jax import lax
from jax.experimental import pallas as pl
from jax.experimental.pallas import tpu as pltpu
from jax.sharding import PartitionSpec as P

MESH = pl.DeviceIdType.MESH
F32, BF16 = jnp.float32, jnp.bfloat16
ITERS = 4
GPB = 8
NX, NY, NZ = 2, 4, 8
G = NX * NY * NZ
DOF, LANES = 192, 256
UPX, LOWX, LOWY, UPY, LOWZ, UPZ, ROWS = 64, 96, 128, 144, 160, 176, 192
SX, SY, SZ, CY = 16, 4, 8, 8
PLANE, ZLINE = 32, 16
LOCAL_GAIN = (3 / 2.125) ** 0.5
NT_DIMS = (((1,), (1,)), ((), ()))


def iota(shape, dim):
    return lax.broadcasted_iota(jnp.int32, shape, dim)


def total(values):
    values = list(values)
    while len(values) > 1:
        pairs = [values[i] + values[i + 1] for i in range(0, len(values) - 1, 2)]
        values = pairs + values[len(pairs) * 2 :]
    return values[0]


def place(i, j):
    i, j = min(i, j), max(i, j)
    return i * 5 - i * (i - 1) // 2 + (j - i)


def entries(row, size):
    lane = iota(row.shape, 1)
    table = {}
    for i in range(size):
        for j in range(i, size):
            table[i, j] = table[j, i] = jnp.sum(
                jnp.where(lane == place(i, j), row, 0.0), axis=1, keepdims=True
            )
    return table


def bilinear(left, table, right):
    return total(
        left[i] * total(table[i, j] * right[j] for j in right) for i in left
    )


def sweeps(table, count, image):
    one = jnp.ones_like(table[0, 0])
    residual, answer, steps = {0: one}, {}, []
    for _ in range(count):
        moved = image(residual)
        projected = bilinear(residual, table, moved)
        energy = bilinear(moved, table, moved)
        step = projected / (energy + 1e-6)
        steps.append(step)
        for i, c in residual.items():
            answer[i] = answer[i] + step * c if i in answer else step * c
        for i, c in moved.items():
            residual[i] = residual[i] - step * c if i in residual else -(step * c)
    return steps, answer, residual


def kernel(body, probe, dens, links, offb, selfb, owner, state_out, adjoint_out, coarse_out,
           x_first, x_rest, faces_first, faces_rest, pick, table, v, su, sc, rp, hot, rr, mp, mps, mz, mzs,
           hs, hr, ps, pr, zs, zr):
    gx, gy, gz = lax.axis_index("gx"), lax.axis_index("gy"), lax.axis_index("gz")
    zh, yc = gx // CY, gx % CY
    me_p = yc * SY + gy
    me_z = zh * SZ + gz
    far = jnp.logical_or(gx == CY - 1, gx == CY)

    def plane_peer(i):
        p = (me_p + 1 + i) % PLANE
        return (zh * CY + p // SY, p % SY, gz)

    def line_peer(i):
        q = (me_z + 1 + i) % ZLINE
        return (q // SZ * CY + yc, gy, q % SZ)

    barrier = pltpu.get_barrier_semaphore()

    def greet_plane(i, _):
        pl.semaphore_signal(barrier, inc=1, device_id=plane_peer(i), device_id_type=MESH)
        return 0

    def greet_line(i, _):
        pl.semaphore_signal(barrier, inc=1, device_id=line_peer(i), device_id_type=MESH)
        return 0

    lax.fori_loop(0, ZLINE - 1, greet_line, 0)

    @pl.when(far)
    def _():
        pl.semaphore_signal(
            barrier, inc=1, device_id=(2 * CY - 1 - gx, gy, gz), device_id_type=MESH
        )

    lax.fori_loop(0, PLANE - 1, greet_plane, 0)

    sends = (
        (gx < SX - 1, (gx + 1, gy, gz)),
        (gx > 0, (gx - 1, gy, gz)),
        (gy < SY - 1, (gx, gy + 1, gz)),
        (gy > 0, (gx, gy - 1, gz)),
        (gz < SZ - 1, (gx, gy, gz + 1)),
        (gz > 0, (gx, gy, gz - 1)),
    )
    lands = ((LOWX, 32), (UPX, 32), (LOWY, 16), (UPY, 16), (LOWZ, 16), (UPZ, 16))
    comes = tuple(sends[d ^ 1][0] for d in range(6))

    def halo(k, d):
        at, size = lands[d]
        x, faces = (x_first, faces_first) if k == 0 else (x_rest.at[k - 1], faces_rest.at[k - 1])
        if d < 2:
            src = x.at[pl.ds(32 - 32 * d, 32)]
        else:
            src = faces.at[pl.ds(16 * (d - 2), 16)]
        return pltpu.make_async_remote_copy(
            src_ref=src,
            dst_ref=x.at[pl.ds(at, size)],
            send_sem=hs.at[k, d],
            recv_sem=hr.at[k, d],
            device_id=sends[d][1],
            device_id_type=MESH,
        )

    def start_halos(k):
        for d in range(6):
            @pl.when(sends[d][0])
            def _():
                halo(k, d).start()

    def wait_halos(k):
        for d in range(6):
            @pl.when(comes[d])
            def _():
                halo(k, d).wait_recv()

    for d in range(6):
        at, size = lands[d]

        @pl.when(jnp.logical_not(comes[d]))
        def _():
            x_first[pl.ds(at, size), :] = jnp.zeros((size, 2 * LANES), BF16)
            x_rest[:, pl.ds(at, size), :] = jnp.zeros((ITERS - 1, size, 4 * LANES), BF16)

    eye8 = iota((8, 8), 0) == iota((8, 8), 1)

    def column(row_of):
        return jnp.concatenate(
            [
                jnp.sum(
                    jnp.where(eye8, jnp.broadcast_to(row_of(a, b).astype(F32), (8, 8)), 0.0),
                    axis=1,
                    keepdims=True,
                )
                for a in range(NX)
                for b in range(NY)
            ],
            axis=0,
        )

    kinds = [column(lambda a, b: links[a, k, b : b + 1, :]) for k in range(7)]
    density = column(lambda a, b: dens[a, b : b + 1, :])
    owners = column(lambda a, b: owner[a, b : b + 1, :])

    scale = density * jnp.sqrt(density)
    eye = iota((DOF, DOF), 0) == iota((DOF, DOF), 1)
    eye_low = jnp.where(eye, 1.0, 0.0).astype(BF16)
    pivots = jnp.zeros((G, DOF), F32)
    table[...] = jnp.zeros(table.shape, BF16)
    for t in range(4):
        block = selfb[t]
        diagonal = jnp.sum(jnp.where(eye, block.astype(F32), 0.0), axis=0, keepdims=True)
        pivots = jnp.where(kinds[6] == float(t), diagonal, pivots)
        upper = lax.dot_general(eye_low, offb[t], NT_DIMS, preferred_element_type=F32)
        table[pl.ds(t * LANES, DOF), pl.ds(0, DOF)] = upper.astype(BF16)
        table[pl.ds((4 + t) * LANES, DOF), pl.ds(0, DOF)] = offb[t]
        table[pl.ds((8 + t) * LANES, DOF), pl.ds(0, DOF)] = block
    rp[...] = jnp.ones((G, LANES), F32)
    rp[:, pl.ds(0, DOF)] = 1.0 / pivots
    sc[...] = jnp.broadcast_to(scale, (G, LANES))
    su[...] = rp[...] * sc[...]

    v[0] = jnp.zeros((2 * G, LANES), F32)
    v[0, pl.ds(0, G), pl.ds(0, DOF)] = body[...].reshape(G, DOF)
    v[0, pl.ds(G, G), pl.ds(0, DOF)] = probe[...].reshape(G, DOF)

    g = iota((G, 1), 0)
    gl, gyy, gzz = g // 32, g // 8 % 4, g % 8
    sources = (
        jnp.where(gl == 0, g + 32, UPX + g - 32),
        jnp.where(gyy < NY - 1, g + 8, UPY + gl * 8 + gzz),
        jnp.where(gzz < NZ - 1, g + 1, UPZ + gl * 4 + gyy),
        jnp.where(gl == 0, LOWX + g, g - 32),
        jnp.where(gyy > 0, g - 8, LOWY + gl * 8 + gzz),
        jnp.where(gzz > 0, g - 1, LOWZ + gl * 4 + gyy),
    )
    across = iota((G, ROWS), 1).astype(F32)
    sources = [s.astype(F32) for s in sources]
    for side in range(2):
        for t in range(4):
            chosen = jnp.zeros((G, ROWS), F32)
            for k in range(3 * side, 3 * side + 3):
                code = jnp.where(kinds[k] == float(t), sources[k], -1.0)
                chosen = jnp.where(across == code, 1.0, chosen)
            pick[pl.ds((4 * side + t) * G, G), :] = chosen.astype(BF16)
    for t in range(4):
        code = jnp.where(kinds[6] == float(t), g.astype(F32), -1.0)
        pick[pl.ds((8 + t) * G, G), :] = jnp.where(across == code, 1.0, 0.0).astype(BF16)

    r = iota((G, 1), 0)
    r16 = r % 16
    face_y = r16 // 8 * 32 + r16 % 8
    face_z = jnp.where(r16 < 8, r16 // 4 * 32 + r16 % 4 * 8, -64)
    face = jnp.where(
        r < 16, face_y + 24, jnp.where(r < 32, face_y, jnp.where(r < 48, face_z + 7, face_z))
    )
    outer = jnp.where(iota((G, G), 1) == face, 1.0, 0.0).astype(BF16)

    def both(a):
        return jnp.concatenate([a, a], axis=0)

    def scaled(field, parts):
        u = field * both(su[...])
        high = u.astype(BF16)
        out = [high[:G], high[G:]]
        if parts == 2:
            low = (u - high.astype(F32)).astype(BF16)
            out += [low[:G], low[G:]]
        return jnp.concatenate(out, axis=1)

    def wide(a, count):
        return [
            jnp.concatenate(
                [a[t * G : (t + 1) * G, f * LANES : (f + 1) * LANES] for t in range(count)],
                axis=1,
            )
            for f in range(a.shape[1] // LANES)
        ]

    def fold(a):
        return a[: 2 * G] + a[2 * G :] if a.shape[0] == 4 * G else a

    def image(sent, width, gain):
        z = jnp.dot(pick[:, pl.ds(0, width)], sent, preferred_element_type=F32)
        off, own = z[: 8 * G], z[8 * G :].astype(BF16)
        if off.shape[1] == 4 * LANES:
            off = off[:, : 2 * LANES] + off[:, 2 * LANES :]
        high = off.astype(BF16)
        low = (off - high.astype(F32)).astype(BF16)
        left = jnp.concatenate(wide(high, 8) + wide(low, 8), axis=0)
        a = jnp.dot(left, table[pl.ds(0, 8 * LANES)], preferred_element_type=F32)
        b = jnp.dot(
            jnp.concatenate(wide(own, 4), axis=0),
            table[pl.ds(8 * LANES, 4 * LANES)],
            preferred_element_type=F32,
        )
        a = fold(a)
        if gain != 1.0:
            a = a * gain
        return (a + fold(b)) * both(sc[...])

    def ship(k, field):
        sent = scaled(field, 1 if k == 0 else 2)
        outside = jnp.dot(outer, sent, preferred_element_type=F32).astype(BF16)
        if k == 0:
            x_first[pl.ds(0, G), :] = sent
            faces_first[...] = outside
        else:
            x_rest[k - 1, pl.ds(0, G), :] = sent
            faces_rest[k - 1] = outside

    def gram(fields, i, j):
        product = fields[i] * fields[j]
        for f in range(2):
            part = jnp.sum(product[f * G : (f + 1) * G], axis=0, keepdims=True)
            rr[pl.ds(f * 16 + place(i, j), 1), :] = part[:, :128] + part[:, 128:]

    def gram_rows():
        sums = jnp.sum(rr[...], axis=1, keepdims=True)
        spot = iota((16, 128), 0) == iota((16, 128), 1)
        return [
            jnp.sum(jnp.where(spot, sums[f * 16 : f * 16 + 16], 0.0), axis=0, keepdims=True)
            for f in range(2)
        ]

    def start_plane(e):
        def one(i, _):
            pltpu.make_async_remote_copy(
                src_ref=mp.at[e], dst_ref=mps.at[e, PLANE - 2 - i],
                send_sem=ps.at[e], recv_sem=pr.at[e],
                device_id=plane_peer(i), device_id_type=MESH,
            ).start()
            return 0

        lax.fori_loop(0, PLANE - 1, one, 0)

    def start_line(e):
        def one(i, _):
            pltpu.make_async_remote_copy(
                src_ref=mz.at[e], dst_ref=mzs.at[e, ZLINE - 2 - i],
                send_sem=zs.at[e], recv_sem=zr.at[e],
                device_id=line_peer(i), device_id_type=MESH,
            ).start()
            return 0

        lax.fori_loop(0, ZLINE - 1, one, 0)

    def wait_all(buffer, sem):
        pltpu.make_async_copy(buffer, buffer, sem).wait()

    rr[...] = jnp.zeros(rr.shape, F32)
    mp[...] = jnp.zeros(mp.shape, F32)
    mz[...] = jnp.zeros(mz.shape, F32)
    ship(0, v[0])

    inner = [v[0]]
    for _ in range(ITERS - 1):
        inner.append(image(scaled(inner[-1], 1), G, LOCAL_GAIN))
    for i in range(ITERS):
        for j in range(i, ITERS):
            gram(inner, i, j)

    half = G * (me_p % 2)
    spread = iota((G, 128), 1) == iota((G, 128), 0) + half

    def as_row(col):
        return jnp.sum(jnp.where(spread, col, 0.0), axis=0, keepdims=True)

    rows = gram_rows()
    mp[0, 0:1, :] = rows[0]
    mp[0, 1:2, :] = rows[1]
    mp[0, 2:3, :] = as_row(owners)
    mp[0, 3:4, :] = as_row(density)

    pl.semaphore_wait(barrier, PLANE - 1 + ZLINE - 1 + far.astype(jnp.int32))
    start_halos(0)
    start_plane(0)
    wait_all(mps.at[0], pr.at[0])
    mz[0] = mp[0] + total(mps[0, i] for i in range(PLANE - 1))
    start_line(0)

    def gathered(e, row):
        parts = [mps[e, i, row : row + 1, :] for i in range(PLANE - 1)]
        parts.append(mp[e, row : row + 1, :])
        return [parts[2 * m] + parts[2 * m + 1] for m in range(PLANE // 2)]

    q = iota((128, 1), 0)
    bins = (((q // 64 * CY + yc) * SY + gy) * SZ + q // 8 % 8) * GPB + q % 8
    bins = bins.astype(F32)
    for m, row in enumerate(gathered(0, 2)):
        hot[:, pl.ds(m * 128, 128)] = jnp.where(row == bins, 1.0, 0.0).astype(BF16)

    def by_block(e, row):
        flat = jnp.concatenate(gathered(e, row), axis=1)
        first = flat.astype(BF16).astype(F32)
        rest = flat - first
        second = rest.astype(BF16).astype(F32)
        third = rest - second
        sub = iota((8, flat.shape[1]), 0)
        split = jnp.where(
            sub == 0, first, jnp.where(sub == 1, second, jnp.where(sub == 2, third, 0.0))
        ).astype(BF16)
        sums = lax.dot_general(split, hot[...], NT_DIMS, preferred_element_type=F32)
        return jnp.sum(sums, axis=0, keepdims=True)

    mz[1, 2:3, :] = by_block(0, 3)

    guess = None
    for k in range(ITERS):
        wait_halos(k)
        moved = image(x_first[...] if k == 0 else x_rest[k - 1], ROWS, 1.0)
        if k == 0:
            wait_all(mzs.at[0], zr.at[0])
            row = mz[0, 0:2, :] + total(mzs[0, i, 0:2, :] for i in range(ZLINE - 1))
            guess, _, _ = sweeps(
                entries(row, ITERS), ITERS - 1, lambda c: {i + 1: e for i, e in c.items()}
            )
            guess = [jnp.where((s > 1e-3) & (s < 1e6), s, 1.0) for s in guess]
        if k < ITERS - 1:
            step = jnp.concatenate(
                [jnp.broadcast_to(guess[k][f : f + 1], (G, 1)) for f in range(2)], axis=0
            )
            v[k + 1] = v[k] - step * moved
            ship(k + 1, v[k + 1])
            start_halos(k + 1)
        else:
            v[k + 1] = moved
        for i in range(k + 2):
            gram(v, i, k + 1)
        if k == 0:
            gram(v, 0, 0)

    rows = gram_rows()
    mp[1, 0:1, :] = rows[0]
    mp[1, 1:2, :] = rows[1]
    start_plane(1)
    wait_all(mps.at[1], pr.at[1])
    mz[1, 0:2, :] = mp[1, 0:2, :] + total(mps[1, i, 0:2, :] for i in range(PLANE - 1))
    start_line(1)
    wait_all(mzs.at[1], zr.at[1])
    row = mz[1] + total(mzs[1, i] for i in range(ZLINE - 1))
    below = row[2:3, :]

    inverse = [1.0 / s for s in guess]

    def newton(c):
        out = {}
        for i, e in c.items():
            if i < ITERS - 1:
                part = e * inverse[i]
                out[i] = out[i] + part if i in out else part
                out[i + 1] = out[i + 1] - part if i + 1 in out else -part
            else:
                out[i + 1] = e
        return out

    _, answer, left = sweeps(entries(row[0:2, :], ITERS + 1), ITERS, newton)

    def combine(coefficients, f):
        return total(
            c[f : f + 1, :] * v[i, pl.ds(f * G, G), :] for i, c in coefficients.items()
        )

    solved = [combine(answer, f) * rp[...] for f in range(2)]
    state_out[...] = solved[0][:, :DOF].reshape(state_out.shape)
    adjoint_out[...] = solved[1][:, :DOF].reshape(adjoint_out.shape)
    applied = {i: (1.0 - c if i == 0 else -c) for i, c in left.items()}
    applied = [combine(applied, f) for f in range(2)]
    bracket = jnp.sum(solved[1] * applied[0] + solved[0] * applied[1], axis=1, keepdims=True)
    weighted = density * (-1.5 * bracket / density)
    mp[2, 0:1, :] = as_row(weighted)
    start_plane(2)
    wait_all(mps.at[2], pr.at[2])
    mz[2, 0:1, :] = by_block(2, 0)
    start_line(2)
    wait_all(mzs.at[2], zr.at[2])
    above = mz[2, 0:1, :] + total(mzs[2, i, 0:1, :] for i in range(ZLINE - 1))
    ratio = jnp.where(below > 0.0, above / below, 0.0)
    mine = iota((8, 128), 1) == iota((8, 128), 0) + 8 * me_z
    col = jnp.sum(jnp.where(mine, ratio, 0.0), axis=1, keepdims=True)
    coarse_out[...] = jnp.sum(jnp.where(eye8, col, 0.0), axis=0, keepdims=True)

    for k in range(ITERS):
        for d in range(6):
            @pl.when(sends[d][0])
            def _():
                halo(k, d).wait_send()
    for e in range(3):
        wait_all(mps.at[e], ps.at[e])
        wait_all(mzs.at[e], zs.at[e])


def local(body_load, probe_load, density, link_types, off_blocks, self_blocks, block_owner):
    vmem = pl.BlockSpec(memory_space=pltpu.VMEM)
    state, adjoint, coarse = pl.pallas_call(
        kernel,
        out_shape=(
            jax.ShapeDtypeStruct(body_load.shape, F32),
            jax.ShapeDtypeStruct(body_load.shape, F32),
            jax.ShapeDtypeStruct((1, GPB), F32),
        ),
        in_specs=[vmem] * 7,
        out_specs=(vmem,) * 3,
        scratch_shapes=[
            pltpu.VMEM((ROWS, 2 * LANES), BF16),
            pltpu.VMEM((ITERS - 1, ROWS, 4 * LANES), BF16),
            pltpu.VMEM((G, 2 * LANES), BF16),
            pltpu.VMEM((ITERS - 1, G, 4 * LANES), BF16),
            pltpu.VMEM((12 * G, ROWS), BF16),
            pltpu.VMEM((12 * LANES, LANES), BF16),
            pltpu.VMEM((ITERS + 1, 2 * G, LANES), F32),
            pltpu.VMEM((G, LANES), F32),
            pltpu.VMEM((G, LANES), F32),
            pltpu.VMEM((G, LANES), F32),
            pltpu.VMEM((128, PLANE * G), BF16),
            pltpu.VMEM((32, 128), F32),
            pltpu.VMEM((3, 4, 128), F32),
            pltpu.VMEM((3, PLANE - 1, 4, 128), F32),
            pltpu.VMEM((3, 4, 128), F32),
            pltpu.VMEM((3, ZLINE - 1, 4, 128), F32),
            pltpu.SemaphoreType.DMA((ITERS, 6)),
            pltpu.SemaphoreType.DMA((ITERS, 6)),
            pltpu.SemaphoreType.DMA((3,)),
            pltpu.SemaphoreType.DMA((3,)),
            pltpu.SemaphoreType.DMA((3,)),
            pltpu.SemaphoreType.DMA((3,)),
        ],
        compiler_params=pltpu.CompilerParams(
            collective_id=0, has_side_effects=True, vmem_limit_bytes=60 << 20
        ),
        name="sweeps",
    )(
        body_load,
        probe_load,
        density,
        jnp.transpose(link_types, (0, 3, 1, 2)),
        off_blocks,
        self_blocks,
        block_owner,
    )
    return state, adjoint, coarse.reshape(GPB)


def solution(mesh):
    in_specs = (
        P("gx", "gy", "gz", None),
        P("gx", "gy", "gz", None),
        P("gx", "gy", "gz"),
        P("gx", "gy", "gz", None),
        P(),
        P(),
        P("gx", "gy", "gz"),
    )
    out_specs = (P("gx", "gy", "gz", None), P("gx", "gy", "gz", None), P(("gx", "gy", "gz")))
    return jax.shard_map(local, mesh=mesh, in_specs=in_specs, out_specs=out_specs, check_vma=False)
```

```python
import functools

import jax
import jax.numpy as jnp
from jax import lax
from jax.experimental import pallas as pl
from jax.experimental.pallas import tpu as pltpu
from jax.sharding import PartitionSpec as P

MESH = pl.DeviceIdType.MESH
F32, BF16 = jnp.float32, jnp.bfloat16
ITERS = 4
GPB = 8
NX, NY, NZ = 2, 4, 8
G = NX * NY * NZ
DOF, LANES = 192, 256
LAYER, DEEP = NY * NZ, 3
ALL = G + DEEP * LAYER
UPX, LOWX, LOWY, UPY, LOWZ, UPZ, ROWS = 64, 192, 224, 272, 320, 352, 384
FACES = (0, 48, 96, 128)
FACE_ROWS = 160
SX, SY, SZ, CY = 16, 4, 8, 8
PLANE, ZLINE = 32, 16
LOCAL_GAIN = (3 / 2.125) ** 0.5
NT_DIMS = (((1,), (1,)), ((), ()))


def iota(shape, dim):
    return lax.broadcasted_iota(jnp.int32, shape, dim)


def total(values):
    values = list(values)
    while len(values) > 1:
        pairs = [values[i] + values[i + 1] for i in range(0, len(values) - 1, 2)]
        values = pairs + values[len(pairs) * 2 :]
    return values[0]


def place(i, j):
    i, j = min(i, j), max(i, j)
    return i * 5 - i * (i - 1) // 2 + (j - i)


def entries(row, size):
    lane = iota(row.shape, 1)
    table = {}
    for i in range(size):
        for j in range(i, size):
            table[i, j] = table[j, i] = jnp.sum(
                jnp.where(lane == place(i, j), row, 0.0), axis=1, keepdims=True
            )
    return table


def bilinear(left, table, right):
    return total(
        left[i] * total(table[i, j] * right[j] for j in right) for i in left
    )


def sweeps(table, count, image):
    one = jnp.ones_like(table[0, 0])
    residual, answer, steps = {0: one}, {}, []
    for _ in range(count):
        moved = image(residual)
        projected = bilinear(residual, table, moved)
        energy = bilinear(moved, table, moved)
        step = projected / (energy + 1e-6)
        steps.append(step)
        for i, c in residual.items():
            answer[i] = answer[i] + step * c if i in answer else step * c
        for i, c in moved.items():
            residual[i] = residual[i] - step * c if i in residual else -(step * c)
    return steps, answer, residual


def kernel(body, probe, dens, links, offb, selfb, owner, state_out, adjoint_out, coarse_out,
           x_first, x_rest, faces_first, faces_rest, low_own, low_far, vg, pick, table, v, su, sc, rp, hot, rr, mp, mps, mz, mzs,
           hs, hr, fs, fr, ps, pr, zs, zr):
    gx, gy, gz = lax.axis_index("gx"), lax.axis_index("gy"), lax.axis_index("gz")
    zh, yc = gx // CY, gx % CY
    me_p = yc * SY + gy
    me_z = zh * SZ + gz
    ghost = jnp.logical_or(gx == CY - 1, gx == CY)
    behind = jnp.logical_or(gx == CY - 2, gx == CY + 1)
    mirror = (gx == CY).astype(jnp.int32)
    across_peer = (2 * CY - 1 - gx, gy, gz)
    behind_peer = (jnp.where(gx == CY + 1, CY - 1, CY), gy, gz)
    greeter = (jnp.where(gx == CY, CY - 2, CY + 1), gy, gz)

    def plane_peer(i):
        p = (me_p + 1 + i) % PLANE
        return (zh * CY + p // SY, p % SY, gz)

    def line_peer(i):
        q = (me_z + 1 + i) % ZLINE
        return (q // SZ * CY + yc, gy, q % SZ)

    barrier = pltpu.get_barrier_semaphore()

    def greet_plane(i, _):
        pl.semaphore_signal(barrier, inc=1, device_id=plane_peer(i), device_id_type=MESH)
        return 0

    def greet_line(i, _):
        pl.semaphore_signal(barrier, inc=1, device_id=line_peer(i), device_id_type=MESH)
        return 0

    lax.fori_loop(0, ZLINE - 1, greet_line, 0)

    @pl.when(ghost)
    def _():
        for peer in (across_peer, greeter):
            pl.semaphore_signal(barrier, inc=1, device_id=peer, device_id_type=MESH)

    @pl.when(behind)
    def _():
        pl.semaphore_signal(barrier, inc=1, device_id=behind_peer, device_id_type=MESH)

    lax.fori_loop(0, PLANE - 1, greet_plane, 0)

    sends = (
        ((gx < SX - 1) & (gx != CY - 1), (gx + 1, gy, gz)),
        ((gx > 0) & (gx != CY), (gx - 1, gy, gz)),
        (gy < SY - 1, (gx, gy + 1, gz)),
        (gy > 0, (gx, gy - 1, gz)),
        (gz < SZ - 1, (gx, gy, gz + 1)),
        (gz > 0, (gx, gy, gz - 1)),
    )
    comes = (
        (gx > 0) & (gx != CY),
        (gx < SX - 1) & (gx != CY - 1),
        gy > 0,
        gy < SY - 1,
        gz > 0,
        gz < SZ - 1,
    )
    lands = (LOWX, jnp.where(gx == CY + 1, LOWX, UPX), LOWY, UPY, LOWZ, UPZ)
    deep_rows = {0: (48, 32), 1: (32, 16), 2: (32, 16), 3: (16, 16)}

    def rows_of(k, d, deep):
        return deep_rows[k][(d - 2) // 2] if deep else 16

    def halo(k, d, deep=False):
        x, faces = (x_first, faces_first) if k == 0 else (x_rest.at[k - 1], faces_rest.at[k - 1])
        if d < 2:
            at = jnp.where(gx == CY, 0, LAYER) if d == 0 else 0
            src = x.at[pl.ds(pl.multiple_of(at, LAYER), LAYER)]
            dst = x.at[pl.ds(pl.multiple_of(lands[d], LAYER), LAYER)]
        else:
            size = rows_of(k, d, deep)
            src = faces.at[pl.ds(FACES[d - 2], size)]
            dst = x.at[pl.ds(lands[d], size)]
        return pltpu.make_async_remote_copy(
            src_ref=src,
            dst_ref=dst,
            send_sem=hs.at[k, d],
            recv_sem=hr.at[k, d],
            device_id=sends[d][1],
            device_id_type=MESH,
        )

    def for_halos(k, ways, conditions, act):
        for d in ways:
            if d < 2:
                @pl.when(conditions[d])
                def _():
                    act(halo(k, d))
            else:
                @pl.when(conditions[d] & ghost)
                def _():
                    act(halo(k, d, True))

                @pl.when(conditions[d] & jnp.logical_not(ghost))
                def _():
                    act(halo(k, d, False))

    def start_halos(k, ways=range(6)):
        for_halos(k, ways, [c for c, _ in sends], lambda copy: copy.start())

    def wait_halos(k, ways=range(6)):
        for_halos(k, ways, comes, lambda copy: copy.wait_recv())

    def far_copy(m):
        first = jnp.where(gx == CY + 1, 0, LAYER)
        src, dst, at, to = (
            (x_first, x_first, LAYER, UPX),
            (x_first, x_first, 0, UPX + LAYER),
            (low_own, low_far, LAYER, 0),
            (low_own, low_far, 0, LAYER),
            (x_first, x_first, first, UPX + 2 * LAYER),
            (x_first, x_first, LAYER - first, UPX + 3 * LAYER),
            (low_own, low_far, first, 2 * LAYER),
        )[m]
        return pltpu.make_async_remote_copy(
            src_ref=src.at[pl.ds(pl.multiple_of(at, LAYER), LAYER)],
            dst_ref=dst.at[pl.ds(to, LAYER)],
            send_sem=fs.at[m],
            recv_sem=fr.at[m],
            device_id=across_peer if m < 4 else behind_peer,
            device_id_type=MESH,
        )

    def clear(at, size, first=True):
        if first:
            x_first[pl.ds(at, size), :] = jnp.zeros((size, 2 * LANES), BF16)
        x_rest[:, pl.ds(at, size), :] = jnp.zeros((ITERS - 1, size, 4 * LANES), BF16)

    clear(UPX + LAYER, 3 * LAYER, False)

    @pl.when(jnp.logical_not(ghost))
    def _():
        x_first[pl.ds(UPX + LAYER, 3 * LAYER), :] = jnp.zeros((3 * LAYER, 2 * LANES), BF16)
        low_far[...] = jnp.zeros(low_far.shape, BF16)
        for at, size in ((LOWY, 48), (UPY, 48), (LOWZ, 32), (UPZ, 32)):
            clear(at + 16, size - 16)

    @pl.when(ghost)
    def _():
        for k in range(1, ITERS):
            for d in range(2, 6):
                size, full = deep_rows[k][(d - 2) // 2], deep_rows[0][(d - 2) // 2]
                if size < full:
                    x_rest[k - 1, pl.ds(lands[d] + size, full - size), :] = jnp.zeros(
                        (full - size, 4 * LANES), BF16
                    )

    for absent, at, size in (
        (gx == 0, LOWX, LAYER),
        (gx == SX - 1, UPX, LAYER),
        (gy == 0, LOWY, 48),
        (gy == SY - 1, UPY, 48),
        (gz == 0, LOWZ, 32),
        (gz == SZ - 1, UPZ, 32),
    ):
        @pl.when(absent)
        def _():
            clear(at, size)

    own = (mirror, 1 - mirror)

    eye8 = iota((8, 8), 0) == iota((8, 8), 1)

    def column(row_of):
        return jnp.concatenate(
            [
                jnp.sum(
                    jnp.where(eye8, jnp.broadcast_to(row_of(own[a], b).astype(F32), (8, 8)), 0.0),
                    axis=1,
                    keepdims=True,
                )
                for a in range(NX)
                for b in range(NY)
            ],
            axis=0,
        )

    kinds = [column(lambda a, b: links[a, k, b : b + 1, :]) for k in range(7)]
    density = column(lambda a, b: dens[a, b : b + 1, :])
    owners = column(lambda a, b: owner[a, b : b + 1, :])

    eye = iota((DOF, DOF), 0) == iota((DOF, DOF), 1)
    eye_low = jnp.where(eye, 1.0, 0.0).astype(BF16)
    diagonals = []
    table[...] = jnp.zeros(table.shape, BF16)
    for t in range(4):
        block = selfb[t]
        diagonals.append(
            jnp.sum(jnp.where(eye, block.astype(F32), 0.0), axis=0, keepdims=True)
        )
        upper = lax.dot_general(eye_low, offb[t], NT_DIMS, preferred_element_type=F32)
        table[pl.ds(t * LANES, DOF), pl.ds(0, DOF)] = upper.astype(BF16)
        table[pl.ds((4 + t) * LANES, DOF), pl.ds(0, DOF)] = offb[t]
        table[pl.ds((8 + t) * LANES, DOF), pl.ds(0, DOF)] = block

    def prepare(at, size, kinds, density):
        scale = density * jnp.sqrt(density)
        pivots = jnp.ones((size, DOF), F32)
        for t in range(4):
            pivots = jnp.where(kinds[6] == float(t), diagonals[t], pivots)
        rows = pl.ds(at, size)
        rp[rows, :] = jnp.ones((size, LANES), F32)
        rp[rows, pl.ds(0, DOF)] = 1.0 / pivots
        sc[rows, :] = jnp.broadcast_to(scale, (size, LANES))
        su[rows, :] = rp[rows, :] * sc[rows, :]
        g = iota((size, 1), 0) + at
        gl, gyy, gzz = g // LAYER, g // NZ % NY, g % NZ
        on = g + LAYER
        back = jnp.where(gl == 0, LOWX + g, g - LAYER)
        sources = (
            jnp.where(mirror == 1, back, on),
            jnp.where(gyy < NY - 1, g + 8, UPY + gl * 8 + gzz),
            jnp.where(gzz < NZ - 1, g + 1, UPZ + gl * 4 + gyy),
            jnp.where(mirror == 1, on, back),
            jnp.where(gyy > 0, g - 8, LOWY + gl * 8 + gzz),
            jnp.where(gzz > 0, g - 1, LOWZ + gl * 4 + gyy),
        )
        across = iota((size, ROWS), 1).astype(F32)
        sources = [a.astype(F32) for a in sources]
        for side in range(2):
            for t in range(4):
                chosen = jnp.zeros((size, ROWS), F32)
                for k in range(3 * side, 3 * side + 3):
                    code = jnp.where(kinds[k] == float(t), sources[k], -1.0)
                    chosen = jnp.where(across == code, 1.0, chosen)
                pick[pl.ds((4 * side + t) * ALL + at, size), :] = chosen.astype(BF16)
        for t in range(4):
            code = jnp.where(kinds[6] == float(t), g.astype(F32), -1.0)
            pick[pl.ds((8 + t) * ALL + at, size), :] = jnp.where(across == code, 1.0, 0.0).astype(
                BF16
            )

    prepare(0, G, kinds, density)

    v[0] = jnp.zeros((2 * G, LANES), F32)
    for a in range(NX):
        for f, load in enumerate((body, probe)):
            v[0, pl.ds(f * G + a * LAYER, LAYER), pl.ds(0, DOF)] = load[own[a]].reshape(LAYER, DOF)

    r = iota((FACE_ROWS, 1), 0)
    along_y, along_z = r % 48, r % 32
    face_y = along_y // 8 * LAYER + along_y % 8
    face_z = along_z // 4 * LAYER + along_z % 4 * 8
    face = jnp.where(
        r < 48, face_y + 24, jnp.where(r < 96, face_y, jnp.where(r < 128, face_z + 7, face_z))
    )
    outer = jnp.where(iota((FACE_ROWS, ALL), 1) == face, 1.0, 0.0).astype(BF16)

    def both(a):
        return jnp.concatenate([a, a], axis=0)

    def scaled(field, factor, parts):
        size = factor.shape[0]
        u = field * both(factor)
        high = u.astype(BF16)
        out = [high[:size], high[size:]]
        if parts == 2:
            low = (u - high.astype(F32)).astype(BF16)
            out += [low[:size], low[size:]]
        return jnp.concatenate(out, axis=1)

    def wide(a, size, count):
        return [
            jnp.concatenate(
                [a[t * size : (t + 1) * size, f * LANES : (f + 1) * LANES] for t in range(count)],
                axis=1,
            )
            for f in range(a.shape[1] // LANES)
        ]

    def image(sent, size, width, gain):
        def fold(a):
            return a[: 2 * size] + a[2 * size :] if a.shape[0] == 4 * size else a

        chosen = jnp.concatenate(
            [pick[pl.ds(t * ALL, size), pl.ds(0, width)] for t in range(12)], axis=0
        )
        z = jnp.dot(chosen, sent, preferred_element_type=F32)
        off, direct = z[: 8 * size], z[8 * size :].astype(BF16)
        if off.shape[1] == 4 * LANES:
            off = off[:, : 2 * LANES] + off[:, 2 * LANES :]
        high = off.astype(BF16)
        low = (off - high.astype(F32)).astype(BF16)
        left = jnp.concatenate(wide(high, size, 8) + wide(low, size, 8), axis=0)
        a = jnp.dot(left, table[pl.ds(0, 8 * LANES)], preferred_element_type=F32)
        b = jnp.dot(
            jnp.concatenate(wide(direct, size, 4), axis=0),
            table[pl.ds(8 * LANES, 4 * LANES)],
            preferred_element_type=F32,
        )
        a = fold(a)
        if gain != 1.0:
            a = a * gain
        return (a + fold(b)) * both(sc[pl.ds(0, size), :])

    def faces_of(sent):
        return jnp.dot(
            outer[:, : sent.shape[0]], sent, preferred_element_type=F32
        ).astype(BF16)

    def ship(k):
        more = (ITERS - k) * LAYER
        sent = scaled(v[k], su[pl.ds(0, G), :], 2)
        x_rest[k - 1, pl.ds(0, G), :] = sent
        beyond = scaled(
            jnp.concatenate([vg[f, pl.ds(0, more), :] for f in range(2)], axis=0),
            su[pl.ds(G, more), :],
            2,
        )

        @pl.when(ghost)
        def _():
            x_rest[k - 1, pl.ds(UPX, more), :] = beyond

        faces_rest[k - 1] = faces_of(jnp.concatenate([sent, beyond], axis=0))

    def gram(fields, i, j):
        product = fields[i] * fields[j]
        for f in range(2):
            part = jnp.sum(product[f * G : (f + 1) * G], axis=0, keepdims=True)
            rr[pl.ds(f * 16 + place(i, j), 1), :] = part[:, :128] + part[:, 128:]

    def gram_rows():
        sums = jnp.sum(rr[...], axis=1, keepdims=True)
        spot = iota((16, 128), 0) == iota((16, 128), 1)
        return [
            jnp.sum(jnp.where(spot, sums[f * 16 : f * 16 + 16], 0.0), axis=0, keepdims=True)
            for f in range(2)
        ]

    def start_plane(e):
        def one(i, _):
            pltpu.make_async_remote_copy(
                src_ref=mp.at[e], dst_ref=mps.at[e, PLANE - 2 - i],
                send_sem=ps.at[e], recv_sem=pr.at[e],
                device_id=plane_peer(i), device_id_type=MESH,
            ).start()
            return 0

        lax.fori_loop(0, PLANE - 1, one, 0)

    def start_line(e):
        def one(i, _):
            pltpu.make_async_remote_copy(
                src_ref=mz.at[e], dst_ref=mzs.at[e, ZLINE - 2 - i],
                send_sem=zs.at[e], recv_sem=zr.at[e],
                device_id=line_peer(i), device_id_type=MESH,
            ).start()
            return 0

        lax.fori_loop(0, ZLINE - 1, one, 0)

    def wait_all(buffer, sem):
        pltpu.make_async_copy(buffer, buffer, sem).wait()

    rr[...] = jnp.zeros(rr.shape, F32)
    mp[...] = jnp.zeros(mp.shape, F32)
    mz[...] = jnp.zeros(mz.shape, F32)
    sent = scaled(v[0], su[pl.ds(0, G), :], 2)
    low_own[...] = sent[:, 2 * LANES :]

    def split3(a):
        first = a.astype(BF16).astype(F32)
        second = (a - first).astype(BF16).astype(F32)
        return [first, second, a - first - second]

    lane = iota((G, LANES), 1)
    notes = sent[:, :LANES].astype(F32)
    for i, col in enumerate(kinds + split3(density)):
        notes = jnp.where(lane == DOF + i, col, notes)
    sent = jnp.concatenate([notes.astype(BF16), sent[:, LANES : 2 * LANES]], axis=1)
    x_first[pl.ds(0, G), :] = sent

    @pl.when(jnp.logical_not(ghost))
    def _():
        faces_first[...] = faces_of(sent)


    inner = [v[0]]
    for _ in range(ITERS - 1):
        inner.append(image(scaled(inner[-1], su[pl.ds(0, G), :], 1), G, G, LOCAL_GAIN))
    for i in range(ITERS):
        for j in range(i, ITERS):
            gram(inner, i, j)

    half = G * (me_p % 2)
    spread = iota((G, 128), 1) == iota((G, 128), 0) + half

    def as_row(col):
        return jnp.sum(jnp.where(spread, col, 0.0), axis=0, keepdims=True)

    rows = gram_rows()
    mp[0, 0:1, :] = rows[0]
    mp[0, 1:2, :] = rows[1]
    mp[0, 2:3, :] = as_row(owners)
    mp[0, 3:4, :] = as_row(density)

    extra = 2 * ghost.astype(jnp.int32) + behind.astype(jnp.int32)
    pl.semaphore_wait(barrier, PLANE - 1 + ZLINE - 1 + extra)

    @pl.when(ghost)
    def _():
        for m in range(4):
            far_copy(m).start()

    @pl.when(behind)
    def _():
        for m in range(4, 7):
            far_copy(m).start()

    start_halos(0, (0, 1))

    @pl.when(jnp.logical_not(ghost))
    def _():
        for d in range(2, 6):
            @pl.when(sends[d][0])
            def _():
                halo(0, d).start()

    start_plane(0)
    wait_all(mps.at[0], pr.at[0])
    mz[0] = mp[0] + total(mps[0, i] for i in range(PLANE - 1))
    start_line(0)

    def gathered(e, row):
        parts = [mps[e, i, row : row + 1, :] for i in range(PLANE - 1)]
        parts.append(mp[e, row : row + 1, :])
        return [parts[2 * m] + parts[2 * m + 1] for m in range(PLANE // 2)]

    q = iota((128, 1), 0)
    bins = (((q // 64 * CY + yc) * SY + gy) * SZ + q // 8 % 8) * GPB + q % 8
    bins = bins.astype(F32)
    for m, row in enumerate(gathered(0, 2)):
        hot[:, pl.ds(m * 128, 128)] = jnp.where(row == bins, 1.0, 0.0).astype(BF16)

    def by_block(e, row):
        flat = jnp.concatenate(gathered(e, row), axis=1)
        first = flat.astype(BF16).astype(F32)
        rest = flat - first
        second = rest.astype(BF16).astype(F32)
        third = rest - second
        sub = iota((8, flat.shape[1]), 0)
        split = jnp.where(
            sub == 0, first, jnp.where(sub == 1, second, jnp.where(sub == 2, third, 0.0))
        ).astype(BF16)
        sums = lax.dot_general(split, hot[...], NT_DIMS, preferred_element_type=F32)
        return jnp.sum(sums, axis=0, keepdims=True)

    mz[1, 2:3, :] = by_block(0, 3)

    wait_halos(0, (0, 1))

    @pl.when(ghost)
    def _():
        for m in (0, 1, 4, 5):
            far_copy(m).wait_recv()
        faces_first[...] = faces_of(x_first[pl.ds(0, ALL), :])
        for d in range(2, 6):
            @pl.when(sends[d][0])
            def _():
                halo(0, d, True).start()

    notes = x_first[pl.ds(UPX, DEEP * LAYER), pl.ds(128, 128)].astype(F32)
    notes = [notes[:, DOF - 128 + i : DOF - 127 + i] for i in range(10)]
    prepare(G, DEEP * LAYER, notes[:7], notes[7] + notes[8] + notes[9])

    guess = None
    for k in range(ITERS):
        wait_halos(k, range(2, 6) if k == 0 else range(6))
        size = ALL - k * LAYER
        moved = image(x_first[...] if k == 0 else x_rest[k - 1], size, ROWS, 1.0)
        ours = jnp.concatenate([moved[:G], moved[size : size + G]], axis=0)
        if k == 0:
            @pl.when(ghost)
            def _():
                for m in (2, 3, 6):
                    far_copy(m).wait_recv()

            beyond = su[pl.ds(G, DEEP * LAYER), :]
            beyond = jnp.where(beyond > 0.0, 1.0 / beyond, 0.0)
            for f in range(2):
                lanes = pl.ds(f * LANES, LANES)
                whole = x_first[pl.ds(UPX, DEEP * LAYER), lanes].astype(F32)
                vg[f] = (whole + low_far[:, lanes].astype(F32)) * beyond
            wait_all(mzs.at[0], zr.at[0])
            row = mz[0, 0:2, :] + total(mzs[0, i, 0:2, :] for i in range(ZLINE - 1))
            guess, _, _ = sweeps(
                entries(row, ITERS), ITERS - 1, lambda c: {i + 1: e for i, e in c.items()}
            )
            guess = [jnp.where((s > 1e-3) & (s < 1e6), s, 1.0) for s in guess]
        if k < ITERS - 1:
            step = jnp.concatenate(
                [jnp.broadcast_to(guess[k][f : f + 1], (G, 1)) for f in range(2)], axis=0
            )
            v[k + 1] = v[k] - step * ours
            for f in range(2):
                more = size - G
                vg[f, pl.ds(0, more), :] = (
                    vg[f, pl.ds(0, more), :]
                    - guess[k][f : f + 1] * moved[f * size + G : (f + 1) * size]
                )
            ship(k + 1)
            start_halos(k + 1)
        else:
            v[k + 1] = ours
        for i in range(k + 2):
            gram(v, i, k + 1)
        if k == 0:
            gram(v, 0, 0)

    rows = gram_rows()
    mp[1, 0:1, :] = rows[0]
    mp[1, 1:2, :] = rows[1]
    start_plane(1)
    wait_all(mps.at[1], pr.at[1])
    mz[1, 0:2, :] = mp[1, 0:2, :] + total(mps[1, i, 0:2, :] for i in range(PLANE - 1))
    start_line(1)
    wait_all(mzs.at[1], zr.at[1])
    row = mz[1] + total(mzs[1, i] for i in range(ZLINE - 1))
    below = row[2:3, :]

    inverse = [1.0 / s for s in guess]

    def newton(c):
        out = {}
        for i, e in c.items():
            if i < ITERS - 1:
                part = e * inverse[i]
                out[i] = out[i] + part if i in out else part
                out[i + 1] = out[i + 1] - part if i + 1 in out else -part
            else:
                out[i + 1] = e
        return out

    _, answer, left = sweeps(entries(row[0:2, :], ITERS + 1), ITERS, newton)

    def combine(coefficients, f):
        return total(
            c[f : f + 1, :] * v[i, pl.ds(f * G, G), :] for i, c in coefficients.items()
        )

    solved = [combine(answer, f) * rp[pl.ds(0, G), :] for f in range(2)]
    for a in range(NX):
        for f, out in enumerate((state_out, adjoint_out)):
            out[own[a]] = solved[f][a * LAYER : (a + 1) * LAYER, :DOF].reshape(NY, NZ, DOF)
    applied = {i: (1.0 - c if i == 0 else -c) for i, c in left.items()}
    applied = [combine(applied, f) for f in range(2)]
    bracket = jnp.sum(solved[1] * applied[0] + solved[0] * applied[1], axis=1, keepdims=True)
    weighted = density * (-1.5 * bracket / density)
    mp[2, 0:1, :] = as_row(weighted)
    start_plane(2)
    wait_all(mps.at[2], pr.at[2])
    mz[2, 0:1, :] = by_block(2, 0)
    start_line(2)
    wait_all(mzs.at[2], zr.at[2])
    above = mz[2, 0:1, :] + total(mzs[2, i, 0:1, :] for i in range(ZLINE - 1))
    ratio = jnp.where(below > 0.0, above / below, 0.0)
    mine = iota((8, 128), 1) == iota((8, 128), 0) + 8 * me_z
    col = jnp.sum(jnp.where(mine, ratio, 0.0), axis=1, keepdims=True)
    coarse_out[...] = jnp.sum(jnp.where(eye8, col, 0.0), axis=0, keepdims=True)

    for k in range(ITERS):
        for_halos(k, range(6), [c for c, _ in sends], lambda copy: copy.wait_send())

    @pl.when(ghost)
    def _():
        for m in range(4):
            far_copy(m).wait_send()

    @pl.when(behind)
    def _():
        for m in range(4, 7):
            far_copy(m).wait_send()

    for e in range(3):
        wait_all(mps.at[e], ps.at[e])
        wait_all(mzs.at[e], zs.at[e])


def local(body_load, probe_load, density, link_types, off_blocks, self_blocks, block_owner):
    vmem = pl.BlockSpec(memory_space=pltpu.VMEM)
    state, adjoint, coarse = pl.pallas_call(
        kernel,
        out_shape=(
            jax.ShapeDtypeStruct(body_load.shape, F32),
            jax.ShapeDtypeStruct(body_load.shape, F32),
            jax.ShapeDtypeStruct((1, GPB), F32),
        ),
        in_specs=[vmem] * 7,
        out_specs=(vmem,) * 3,
        scratch_shapes=[
            pltpu.VMEM((ROWS, 2 * LANES), BF16),
            pltpu.VMEM((ITERS - 1, ROWS, 4 * LANES), BF16),
            pltpu.VMEM((FACE_ROWS, 2 * LANES), BF16),
            pltpu.VMEM((ITERS - 1, FACE_ROWS, 4 * LANES), BF16),
            pltpu.VMEM((G, 2 * LANES), BF16),
            pltpu.VMEM((DEEP * LAYER, 2 * LANES), BF16),
            pltpu.VMEM((2, DEEP * LAYER, LANES), F32),
            pltpu.VMEM((12 * ALL, ROWS), BF16),
            pltpu.VMEM((12 * LANES, LANES), BF16),
            pltpu.VMEM((ITERS + 1, 2 * G, LANES), F32),
            pltpu.VMEM((ALL, LANES), F32),
            pltpu.VMEM((ALL, LANES), F32),
            pltpu.VMEM((ALL, LANES), F32),
            pltpu.VMEM((128, PLANE * G), BF16),
            pltpu.VMEM((32, 128), F32),
            pltpu.VMEM((3, 4, 128), F32),
            pltpu.VMEM((3, PLANE - 1, 4, 128), F32),
            pltpu.VMEM((3, 4, 128), F32),
            pltpu.VMEM((3, ZLINE - 1, 4, 128), F32),
            pltpu.SemaphoreType.DMA((ITERS, 6)),
            pltpu.SemaphoreType.DMA((ITERS, 6)),
            pltpu.SemaphoreType.DMA((7,)),
            pltpu.SemaphoreType.DMA((7,)),
            pltpu.SemaphoreType.DMA((3,)),
            pltpu.SemaphoreType.DMA((3,)),
            pltpu.SemaphoreType.DMA((3,)),
            pltpu.SemaphoreType.DMA((3,)),
        ],
        compiler_params=pltpu.CompilerParams(
            collective_id=0, has_side_effects=True, vmem_limit_bytes=60 << 20
        ),
        name="sweeps",
    )(
        body_load,
        probe_load,
        density,
        jnp.transpose(link_types, (0, 3, 1, 2)),
        off_blocks,
        self_blocks,
        block_owner,
    )
    return state, adjoint, coarse.reshape(GPB)


def solution(mesh):
    in_specs = (
        P("gx", "gy", "gz", None),
        P("gx", "gy", "gz", None),
        P("gx", "gy", "gz"),
        P("gx", "gy", "gz", None),
        P(),
        P(),
        P("gx", "gy", "gz"),
    )
    out_specs = (P("gx", "gy", "gz", None), P("gx", "gy", "gz", None), P(("gx", "gy", "gz")))
    return jax.shard_map(local, mesh=mesh, in_specs=in_specs, out_specs=out_specs, check_vma=False)
```

```python
import functools

import jax
import jax.numpy as jnp
from jax import lax
from jax.experimental import pallas as pl
from jax.experimental.pallas import tpu as pltpu
from jax.sharding import PartitionSpec as P

MESH = pl.DeviceIdType.MESH
F32, BF16 = jnp.float32, jnp.bfloat16
ITERS = 4
GPB = 8
NX, NY, NZ = 2, 4, 8
G = NX * NY * NZ
DOF, LANES = 192, 256
LAYER, DEEP = NY * NZ, 3
ALL = G + DEEP * LAYER
UPX, LOWX, LOWY, UPY, LOWZ, UPZ, ROWS = 64, 192, 224, 272, 320, 352, 384
FACES = (0, 48, 96, 128)
FACE_ROWS = 160
OUT, SOURCES = 96, 256
SX, SY, SZ, CY = 16, 4, 8, 8
PLANE, ZLINE = 32, 16
LOCAL_GAIN = (3 / 2.125) ** 0.5
NT_DIMS = (((1,), (1,)), ((), ()))


def iota(shape, dim):
    return lax.broadcasted_iota(jnp.int32, shape, dim)


def total(values):
    values = list(values)
    while len(values) > 1:
        pairs = [values[i] + values[i + 1] for i in range(0, len(values) - 1, 2)]
        values = pairs + values[len(pairs) * 2 :]
    return values[0]


def place(i, j):
    i, j = min(i, j), max(i, j)
    return i * 5 - i * (i - 1) // 2 + (j - i)


def entries(row, size):
    lane = iota(row.shape, 1)
    table = {}
    for i in range(size):
        for j in range(i, size):
            table[i, j] = table[j, i] = jnp.sum(
                jnp.where(lane == place(i, j), row, 0.0), axis=1, keepdims=True
            )
    return table


def bilinear(left, table, right):
    return total(
        left[i] * total(table[i, j] * right[j] for j in right) for i in left
    )


def sweeps(table, count, image):
    one = jnp.ones_like(table[0, 0])
    residual, answer, steps = {0: one}, {}, []
    for _ in range(count):
        moved = image(residual)
        projected = bilinear(residual, table, moved)
        energy = bilinear(moved, table, moved)
        step = projected / (energy + 1e-6)
        steps.append(step)
        for i, c in residual.items():
            answer[i] = answer[i] + step * c if i in answer else step * c
        for i, c in moved.items():
            residual[i] = residual[i] - step * c if i in residual else -(step * c)
    return steps, answer, residual


def kernel(body, probe, dens, links, offb, selfb, owner, state_out, adjoint_out, coarse_out,
           x_one, x_two, faces_one, faces_two, vg, pick, table, v, su, sc, rp, hot, rr, mp, mps, mz, mzs,
           hs, hr, fs, fr, ps, pr, zs, zr):
    gx, gy, gz = lax.axis_index("gx"), lax.axis_index("gy"), lax.axis_index("gz")
    zh, yc = gx // CY, gx % CY
    me_p = yc * SY + gy
    me_z = zh * SZ + gz
    ghost = jnp.logical_or(gx == CY - 1, gx == CY)
    behind = jnp.logical_or(gx == CY - 2, gx == CY + 1)
    mirror = (gx == CY).astype(jnp.int32)
    across_peer = (2 * CY - 1 - gx, gy, gz)
    behind_peer = (jnp.where(gx == CY + 1, CY - 1, CY), gy, gz)
    greeter = (jnp.where(gx == CY, CY - 2, CY + 1), gy, gz)

    def plane_peer(i):
        p = (me_p + 1 + i) % PLANE
        return (zh * CY + p // SY, p % SY, gz)

    def line_peer(i):
        q = (me_z + 1 + i) % ZLINE
        return (q // SZ * CY + yc, gy, q % SZ)

    barrier = pltpu.get_barrier_semaphore()

    def greet_plane(i, _):
        pl.semaphore_signal(barrier, inc=1, device_id=plane_peer(i), device_id_type=MESH)
        return 0

    def greet_line(i, _):
        pl.semaphore_signal(barrier, inc=1, device_id=line_peer(i), device_id_type=MESH)
        return 0

    lax.fori_loop(0, ZLINE - 1, greet_line, 0)

    @pl.when(ghost)
    def _():
        for peer in (across_peer, greeter):
            pl.semaphore_signal(barrier, inc=1, device_id=peer, device_id_type=MESH)

    @pl.when(behind)
    def _():
        pl.semaphore_signal(barrier, inc=1, device_id=behind_peer, device_id_type=MESH)

    lax.fori_loop(0, PLANE - 1, greet_plane, 0)

    sends = (
        ((gx < SX - 1) & (gx != CY - 1), (gx + 1, gy, gz)),
        ((gx > 0) & (gx != CY), (gx - 1, gy, gz)),
        (gy < SY - 1, (gx, gy + 1, gz)),
        (gy > 0, (gx, gy - 1, gz)),
        (gz < SZ - 1, (gx, gy, gz + 1)),
        (gz > 0, (gx, gy, gz - 1)),
    )
    comes = (
        (gx > 0) & (gx != CY),
        (gx < SX - 1) & (gx != CY - 1),
        gy > 0,
        gy < SY - 1,
        gz > 0,
        gz < SZ - 1,
    )
    lands = (LOWX, jnp.where(gx == CY + 1, LOWX, UPX), LOWY, UPY, LOWZ, UPZ)
    deep_rows = {0: (48, 32), 1: (32, 16), 2: (32, 16), 3: (16, 16)}

    def rows_of(k, d, deep):
        return deep_rows[k][(d - 2) // 2] if deep else 16

    def halo(k, d, deep=False):
        x = x_one.at[k] if k < 2 else x_two.at[k - 2]
        faces = faces_one.at[k] if k < 2 else faces_two.at[k - 2]
        if d < 2:
            at = jnp.where(gx == CY, 0, LAYER) if d == 0 else 0
            src = x.at[pl.ds(pl.multiple_of(at, LAYER), LAYER)]
            dst = x.at[pl.ds(pl.multiple_of(lands[d], LAYER), LAYER)]
        else:
            size = rows_of(k, d, deep)
            src = faces.at[pl.ds(FACES[d - 2], size)]
            dst = x.at[pl.ds(lands[d], size)]
        return pltpu.make_async_remote_copy(
            src_ref=src,
            dst_ref=dst,
            send_sem=hs.at[k, d],
            recv_sem=hr.at[k, d],
            device_id=sends[d][1],
            device_id_type=MESH,
        )

    def for_halos(k, ways, conditions, act):
        for d in ways:
            if d < 2:
                @pl.when(conditions[d])
                def _():
                    act(halo(k, d))
            else:
                @pl.when(conditions[d] & ghost)
                def _():
                    act(halo(k, d, True))

                @pl.when(conditions[d] & jnp.logical_not(ghost))
                def _():
                    act(halo(k, d, False))

    def start_halos(k, ways=range(6)):
        for_halos(k, ways, [c for c, _ in sends], lambda copy: copy.start())

    def wait_halos(k, ways=range(6)):
        for_halos(k, ways, comes, lambda copy: copy.wait_recv())

    def far_copy(m):
        first = jnp.where(gx == CY + 1, 0, LAYER)
        at = (LAYER, 0, first, LAYER - first)[m]
        return pltpu.make_async_remote_copy(
            src_ref=x_one.at[0, pl.ds(pl.multiple_of(at, LAYER), LAYER)],
            dst_ref=x_one.at[0, pl.ds(UPX + m * LAYER, LAYER)],
            send_sem=fs.at[m],
            recv_sem=fr.at[m],
            device_id=across_peer if m < 2 else behind_peer,
            device_id_type=MESH,
        )

    def clear(at, size, first=True):
        for k in range(0 if first else 1, 2):
            x_one[k, pl.ds(at, size), :] = jnp.zeros((size, 2 * LANES), BF16)
        x_two[:, pl.ds(at, size), :] = jnp.zeros((2, size, 4 * LANES), BF16)

    clear(UPX + LAYER, 3 * LAYER, False)

    @pl.when(jnp.logical_not(ghost))
    def _():
        x_one[0, pl.ds(UPX + LAYER, 3 * LAYER), :] = jnp.zeros((3 * LAYER, 2 * LANES), BF16)
        for at, size in ((LOWY, 48), (UPY, 48), (LOWZ, 32), (UPZ, 32)):
            clear(at + 16, size - 16)

    @pl.when(ghost)
    def _():
        for k in range(1, ITERS):
            for d in range(2, 6):
                size, full = deep_rows[k][(d - 2) // 2], deep_rows[0][(d - 2) // 2]
                if size < full:
                    rest = pl.ds(lands[d] + size, full - size)
                    if k < 2:
                        x_one[k, rest, :] = jnp.zeros((full - size, 2 * LANES), BF16)
                    else:
                        x_two[k - 2, rest, :] = jnp.zeros((full - size, 4 * LANES), BF16)

    for absent, at, size in (
        (gx == 0, LOWX, LAYER),
        (gx == SX - 1, UPX, LAYER),
        (gy == 0, LOWY, 48),
        (gy == SY - 1, UPY, 48),
        (gz == 0, LOWZ, 32),
        (gz == SZ - 1, UPZ, 32),
    ):
        @pl.when(absent)
        def _():
            clear(at, size)

    own = (mirror, 1 - mirror)

    eye8 = iota((8, 8), 0) == iota((8, 8), 1)

    def column(row_of):
        return jnp.concatenate(
            [
                jnp.sum(
                    jnp.where(eye8, jnp.broadcast_to(row_of(own[a], b).astype(F32), (8, 8)), 0.0),
                    axis=1,
                    keepdims=True,
                )
                for a in range(NX)
                for b in range(NY)
            ],
            axis=0,
        )

    kinds = [column(lambda a, b: links[a, k, b : b + 1, :]) for k in range(7)]
    density = column(lambda a, b: dens[a, b : b + 1, :])
    owners = column(lambda a, b: owner[a, b : b + 1, :])

    eye = iota((DOF, DOF), 0) == iota((DOF, DOF), 1)
    eye_low = jnp.where(eye, 1.0, 0.0).astype(BF16)
    diagonals = []
    table[...] = jnp.zeros(table.shape, BF16)
    for t in range(4):
        block = selfb[t]
        diagonals.append(
            jnp.sum(jnp.where(eye, block.astype(F32), 0.0), axis=0, keepdims=True)
        )
        upper = lax.dot_general(eye_low, offb[t], NT_DIMS, preferred_element_type=F32)
        table[pl.ds(t * LANES, DOF), pl.ds(0, DOF)] = upper.astype(BF16)
        table[pl.ds((4 + t) * LANES, DOF), pl.ds(0, DOF)] = offb[t]
        table[pl.ds((8 + t) * LANES, DOF), pl.ds(0, DOF)] = block

    def prepare(at, size, kinds, density):
        scale = density * jnp.sqrt(density)
        pivots = jnp.ones((size, DOF), F32)
        for t in range(4):
            pivots = jnp.where(kinds[6] == float(t), diagonals[t], pivots)
        rows = pl.ds(at, size)
        rp[rows, :] = jnp.ones((size, LANES), F32)
        rp[rows, pl.ds(0, DOF)] = 1.0 / pivots
        sc[rows, :] = jnp.broadcast_to(scale, (size, LANES))
        su[rows, :] = rp[rows, :] * sc[rows, :]
        g = iota((size, 1), 0) + at
        gl, here, gyy, gzz = g // LAYER, g % LAYER, g // NZ % NY, g % NZ
        on, back = here + 2 * LAYER, here
        y, z = OUT + gl * NZ + gzz, OUT + gl * NY + gyy
        sources = (
            jnp.where(mirror == 1, back, on),
            jnp.where(gyy < NY - 1, here + LAYER + 8, y + FACES[1]),
            jnp.where(gzz < NZ - 1, here + LAYER + 1, z + FACES[3]),
            jnp.where(mirror == 1, on, back),
            jnp.where(gyy > 0, here + LAYER - 8, y + FACES[0]),
            jnp.where(gzz > 0, here + LAYER - 1, z + FACES[2]),
        )
        across = iota((size, SOURCES), 1).astype(F32)
        sources = [a.astype(F32) for a in sources]
        for side in range(2):
            for t in range(4):
                chosen = jnp.zeros((size, SOURCES), F32)
                for k in range(3 * side, 3 * side + 3):
                    code = jnp.where(kinds[k] == float(t), sources[k], -1.0)
                    chosen = jnp.where(across == code, 1.0, chosen)
                chosen = chosen.astype(BF16)
                for i in range(size // LAYER):
                    pick[at // LAYER + i, pl.ds((4 * side + t) * LAYER, LAYER), :] = chosen[
                        i * LAYER : (i + 1) * LAYER
                    ]

    prepare(0, G, kinds, density)

    v[0] = jnp.zeros((2 * G, LANES), F32)
    for a in range(NX):
        for f, load in enumerate((body, probe)):
            v[0, pl.ds(f * G + a * LAYER, LAYER), pl.ds(0, DOF)] = load[own[a]].reshape(LAYER, DOF)

    r = iota((FACE_ROWS, 1), 0)
    along_y, along_z = r % 48, r % 32
    face_y = along_y // 8 * LAYER + along_y % 8
    face_z = along_z // 4 * LAYER + along_z % 4 * 8
    face = jnp.where(
        r < 48, face_y + 24, jnp.where(r < 96, face_y, jnp.where(r < 128, face_z + 7, face_z))
    )
    outer = jnp.where(iota((FACE_ROWS, ALL), 1) == face, 1.0, 0.0).astype(BF16)

    def both(a):
        return jnp.concatenate([a, a], axis=0)

    def scaled(field, factor, parts):
        size = factor.shape[0]
        u = field * both(factor)
        high = u.astype(BF16)
        out = [high[:size], high[size:]]
        if parts == 2:
            low = (u - high.astype(F32)).astype(BF16)
            out += [low[:size], low[size:]]
        return out

    def fold(a, size):
        return a[: 2 * size] + a[2 * size :] if a.shape[0] == 4 * size else a

    def straight(parts, kind):
        size = kind.shape[0]
        masks = [jnp.broadcast_to(kind == float(t), (size, LANES)) for t in range(4)]
        left = []
        for part in parts:
            part = part.astype(F32)
            left.append(
                jnp.concatenate([jnp.where(m, part, 0.0).astype(BF16) for m in masks], axis=1)
            )
        left = jnp.concatenate(left, axis=0)
        return fold(
            jnp.dot(left, table[pl.ds(8 * LANES, 4 * LANES)], preferred_element_type=F32), size
        )

    def coupled(sources):
        size = len(sources) * LAYER
        highs, lows = ([], []), ([], [])
        for i, source in enumerate(sources):
            z = jnp.dot(pick[i], source, preferred_element_type=F32)
            if z.shape[1] == 4 * LANES:
                z = z[:, : 2 * LANES] + z[:, 2 * LANES :]
            high = z.astype(BF16)
            low = (z - high.astype(F32)).astype(BF16)
            for f in range(2):
                for a, out in ((high, highs), (low, lows)):
                    out[f].append(
                        jnp.concatenate(
                            [
                                a[t * LAYER : (t + 1) * LAYER, f * LANES : (f + 1) * LANES]
                                for t in range(8)
                            ],
                            axis=1,
                        )
                    )
        left = jnp.concatenate(highs[0] + highs[1] + lows[0] + lows[1], axis=0)
        return fold(jnp.dot(left, table[pl.ds(0, 8 * LANES)], preferred_element_type=F32), size)

    def sources_of(k, layers):
        def rows(at, size):
            return x_one[k, pl.ds(at, size), :] if k < 2 else x_two[k - 2, pl.ds(at, size), :]

        outside = rows(LOWY, FACE_ROWS)
        out = []
        for i in range(layers):
            near = (
                [rows(LOWX, LAYER), rows(0, 2 * LAYER)]
                if i == 0
                else [rows((i - 1) * LAYER, 3 * LAYER)]
            )
            out.append(jnp.concatenate(near + [outside], axis=0))
        return out

    def faces_of(sent):
        return jnp.dot(
            outer[:, : sent.shape[0]], sent, preferred_element_type=F32
        ).astype(BF16)

    def ship(k):
        more = (ITERS - k) * LAYER
        own_parts = scaled(v[k], su[pl.ds(0, G), :], 1 if k < 2 else 2)
        far_parts = scaled(
            jnp.concatenate([vg[f, pl.ds(0, more), :] for f in range(2)], axis=0),
            su[pl.ds(G, more), :],
            1 if k < 2 else 2,
        )
        sent = jnp.concatenate(own_parts, axis=1)
        beyond = jnp.concatenate(far_parts, axis=1)
        x, i = (x_one, k) if k < 2 else (x_two, k - 2)
        x[i, pl.ds(0, G), :] = sent

        @pl.when(ghost)
        def _():
            x[i, pl.ds(UPX, more), :] = beyond

        (faces_one if k < 2 else faces_two)[i] = faces_of(
            jnp.concatenate([sent, beyond], axis=0)
        )
        last = more - LAYER
        return [
            jnp.concatenate([a, b[:last]], axis=0) if last else a
            for a, b in zip(own_parts, far_parts)
        ]

    def gram(fields, i, j):
        product = fields[i] * fields[j]
        for f in range(2):
            part = jnp.sum(product[f * G : (f + 1) * G], axis=0, keepdims=True)
            rr[pl.ds(f * 16 + place(i, j), 1), :] = part[:, :128] + part[:, 128:]

    def gram_rows():
        sums = jnp.sum(rr[...], axis=1, keepdims=True)
        spot = iota((16, 128), 0) == iota((16, 128), 1)
        return [
            jnp.sum(jnp.where(spot, sums[f * 16 : f * 16 + 16], 0.0), axis=0, keepdims=True)
            for f in range(2)
        ]

    def start_plane(e):
        def one(i, _):
            pltpu.make_async_remote_copy(
                src_ref=mp.at[e], dst_ref=mps.at[e, PLANE - 2 - i],
                send_sem=ps.at[e], recv_sem=pr.at[e],
                device_id=plane_peer(i), device_id_type=MESH,
            ).start()
            return 0

        lax.fori_loop(0, PLANE - 1, one, 0)

    def start_line(e):
        def one(i, _):
            pltpu.make_async_remote_copy(
                src_ref=mz.at[e], dst_ref=mzs.at[e, ZLINE - 2 - i],
                send_sem=zs.at[e], recv_sem=zr.at[e],
                device_id=line_peer(i), device_id_type=MESH,
            ).start()
            return 0

        lax.fori_loop(0, ZLINE - 1, one, 0)

    def wait_all(buffer, sem):
        pltpu.make_async_copy(buffer, buffer, sem).wait()

    rr[...] = jnp.zeros(rr.shape, F32)
    mp[...] = jnp.zeros(mp.shape, F32)
    mz[...] = jnp.zeros(mz.shape, F32)
    sent = scaled(v[0], su[pl.ds(0, G), :], 1)

    def split3(a):
        first = a.astype(BF16).astype(F32)
        second = (a - first).astype(BF16).astype(F32)
        return [first, second, a - first - second]

    lane = iota((G, LANES), 1)
    notes = sent[0].astype(F32)
    for i, col in enumerate(kinds + split3(density)):
        notes = jnp.where(lane == DOF + i, col, notes)
    sent = jnp.concatenate([notes.astype(BF16), sent[1]], axis=1)
    x_one[0, pl.ds(0, G), :] = sent

    @pl.when(jnp.logical_not(ghost))
    def _():
        faces_one[0] = faces_of(sent)


    inner = [v[0]]
    for _ in range(ITERS - 1):
        parts = scaled(inner[-1], su[pl.ds(0, G), :], 1)
        near = jnp.concatenate(parts, axis=1)

        def empty(size):
            return jnp.zeros((size, 2 * LANES), BF16)

        moved = LOCAL_GAIN * coupled(
            [
                jnp.concatenate([empty(LAYER), near, empty(FACE_ROWS)], axis=0),
                jnp.concatenate([near, empty(LAYER + FACE_ROWS)], axis=0),
            ]
        )
        inner.append((moved + straight(parts, kinds[6])) * both(sc[pl.ds(0, G), :]))
    for i in range(ITERS):
        for j in range(i, ITERS):
            gram(inner, i, j)

    half = G * (me_p % 2)
    spread = iota((G, 128), 1) == iota((G, 128), 0) + half

    def as_row(col):
        return jnp.sum(jnp.where(spread, col, 0.0), axis=0, keepdims=True)

    rows = gram_rows()
    mp[0, 0:1, :] = rows[0]
    mp[0, 1:2, :] = rows[1]
    mp[0, 2:3, :] = as_row(owners)
    mp[0, 3:4, :] = as_row(density)

    extra = 2 * ghost.astype(jnp.int32) + behind.astype(jnp.int32)
    pl.semaphore_wait(barrier, PLANE - 1 + ZLINE - 1 + extra)

    @pl.when(ghost)
    def _():
        for m in range(2):
            far_copy(m).start()

    @pl.when(behind)
    def _():
        for m in range(2, 4):
            far_copy(m).start()

    start_halos(0, (0, 1))

    @pl.when(jnp.logical_not(ghost))
    def _():
        for d in range(2, 6):
            @pl.when(sends[d][0])
            def _():
                halo(0, d).start()

    start_plane(0)
    wait_all(mps.at[0], pr.at[0])
    mz[0] = mp[0] + total(mps[0, i] for i in range(PLANE - 1))
    start_line(0)

    def gathered(e, row):
        parts = [mps[e, i, row : row + 1, :] for i in range(PLANE - 1)]
        parts.append(mp[e, row : row + 1, :])
        return [parts[2 * m] + parts[2 * m + 1] for m in range(PLANE // 2)]

    q = iota((128, 1), 0)
    bins = (((q // 64 * CY + yc) * SY + gy) * SZ + q // 8 % 8) * GPB + q % 8
    bins = bins.astype(F32)
    for m, row in enumerate(gathered(0, 2)):
        hot[:, pl.ds(m * 128, 128)] = jnp.where(row == bins, 1.0, 0.0).astype(BF16)

    def by_block(e, row):
        flat = jnp.concatenate(gathered(e, row), axis=1)
        first = flat.astype(BF16).astype(F32)
        rest = flat - first
        second = rest.astype(BF16).astype(F32)
        third = rest - second
        sub = iota((8, flat.shape[1]), 0)
        split = jnp.where(
            sub == 0, first, jnp.where(sub == 1, second, jnp.where(sub == 2, third, 0.0))
        ).astype(BF16)
        sums = lax.dot_general(split, hot[...], NT_DIMS, preferred_element_type=F32)
        return jnp.sum(sums, axis=0, keepdims=True)

    mz[1, 2:3, :] = by_block(0, 3)

    wait_halos(0, (0, 1))

    @pl.when(ghost)
    def _():
        for m in range(4):
            far_copy(m).wait_recv()
        faces_one[0] = faces_of(x_one[0, pl.ds(0, ALL), :])
        for d in range(2, 6):
            @pl.when(sends[d][0])
            def _():
                halo(0, d, True).start()

    notes = x_one[0, pl.ds(UPX, DEEP * LAYER), pl.ds(128, 128)].astype(F32)
    notes = [notes[:, DOF - 128 + i : DOF - 127 + i] for i in range(10)]
    prepare(G, DEEP * LAYER, notes[:7], notes[7] + notes[8] + notes[9])
    kind = jnp.concatenate([kinds[6], notes[6]], axis=0)
    beyond = su[pl.ds(G, DEEP * LAYER), :]
    beyond = jnp.where(beyond > 0.0, 1.0 / beyond, 0.0)
    parts = []
    for f in range(2):
        parts.append(x_one[0, pl.ds(0, ALL), pl.ds(f * LANES, LANES)])
        vg[f] = parts[f][G:].astype(F32) * beyond

    guess = None
    for k in range(ITERS):
        size = ALL - k * LAYER
        alone = straight(parts, kind[:size])
        wait_halos(k, range(2, 6) if k == 0 else range(6))
        moved = (coupled(sources_of(k, size // LAYER)) + alone) * both(sc[pl.ds(0, size), :])
        ours = jnp.concatenate([moved[:G], moved[size : size + G]], axis=0)
        if k == 0:
            wait_all(mzs.at[0], zr.at[0])
            row = mz[0, 0:2, :] + total(mzs[0, i, 0:2, :] for i in range(ZLINE - 1))
            guess, _, _ = sweeps(
                entries(row, ITERS), ITERS - 1, lambda c: {i + 1: e for i, e in c.items()}
            )
            guess = [jnp.where((s > 1e-3) & (s < 1e6), s, 1.0) for s in guess]
        if k < ITERS - 1:
            step = jnp.concatenate(
                [jnp.broadcast_to(guess[k][f : f + 1], (G, 1)) for f in range(2)], axis=0
            )
            v[k + 1] = v[k] - step * ours
            for f in range(2):
                more = size - G
                vg[f, pl.ds(0, more), :] = (
                    vg[f, pl.ds(0, more), :]
                    - guess[k][f : f + 1] * moved[f * size + G : (f + 1) * size]
                )
            parts = ship(k + 1)
            start_halos(k + 1)
        else:
            v[k + 1] = ours
        for i in range(k + 2):
            gram(v, i, k + 1)
        if k == 0:
            gram(v, 0, 0)

    rows = gram_rows()
    mp[1, 0:1, :] = rows[0]
    mp[1, 1:2, :] = rows[1]
    start_plane(1)
    wait_all(mps.at[1], pr.at[1])
    mz[1, 0:2, :] = mp[1, 0:2, :] + total(mps[1, i, 0:2, :] for i in range(PLANE - 1))
    start_line(1)
    wait_all(mzs.at[1], zr.at[1])
    row = mz[1] + total(mzs[1, i] for i in range(ZLINE - 1))
    below = row[2:3, :]

    inverse = [1.0 / s for s in guess]

    def newton(c):
        out = {}
        for i, e in c.items():
            if i < ITERS - 1:
                part = e * inverse[i]
                out[i] = out[i] + part if i in out else part
                out[i + 1] = out[i + 1] - part if i + 1 in out else -part
            else:
                out[i + 1] = e
        return out

    _, answer, left = sweeps(entries(row[0:2, :], ITERS + 1), ITERS, newton)

    def combine(coefficients, f):
        return total(
            c[f : f + 1, :] * v[i, pl.ds(f * G, G), :] for i, c in coefficients.items()
        )

    solved = [combine(answer, f) * rp[pl.ds(0, G), :] for f in range(2)]
    for a in range(NX):
        for f, out in enumerate((state_out, adjoint_out)):
            out[own[a]] = solved[f][a * LAYER : (a + 1) * LAYER, :DOF].reshape(NY, NZ, DOF)
    applied = {i: (1.0 - c if i == 0 else -c) for i, c in left.items()}
    applied = [combine(applied, f) for f in range(2)]
    bracket = jnp.sum(solved[1] * applied[0] + solved[0] * applied[1], axis=1, keepdims=True)
    weighted = density * (-1.5 * bracket / density)
    mp[2, 0:1, :] = as_row(weighted)
    start_plane(2)
    wait_all(mps.at[2], pr.at[2])
    mz[2, 0:1, :] = by_block(2, 0)
    start_line(2)
    wait_all(mzs.at[2], zr.at[2])
    above = mz[2, 0:1, :] + total(mzs[2, i, 0:1, :] for i in range(ZLINE - 1))
    ratio = jnp.where(below > 0.0, above / below, 0.0)
    mine = iota((8, 128), 1) == iota((8, 128), 0) + 8 * me_z
    col = jnp.sum(jnp.where(mine, ratio, 0.0), axis=1, keepdims=True)
    coarse_out[...] = jnp.sum(jnp.where(eye8, col, 0.0), axis=0, keepdims=True)

    for k in range(ITERS):
        for_halos(k, range(6), [c for c, _ in sends], lambda copy: copy.wait_send())

    @pl.when(ghost)
    def _():
        for m in range(2):
            far_copy(m).wait_send()

    @pl.when(behind)
    def _():
        for m in range(2, 4):
            far_copy(m).wait_send()

    for e in range(3):
        wait_all(mps.at[e], ps.at[e])
        wait_all(mzs.at[e], zs.at[e])


def local(body_load, probe_load, density, link_types, off_blocks, self_blocks, block_owner):
    vmem = pl.BlockSpec(memory_space=pltpu.VMEM)
    state, adjoint, coarse = pl.pallas_call(
        kernel,
        out_shape=(
            jax.ShapeDtypeStruct(body_load.shape, F32),
            jax.ShapeDtypeStruct(body_load.shape, F32),
            jax.ShapeDtypeStruct((1, GPB), F32),
        ),
        in_specs=[vmem] * 7,
        out_specs=(vmem,) * 3,
        scratch_shapes=[
            pltpu.VMEM((2, ROWS, 2 * LANES), BF16),
            pltpu.VMEM((2, ROWS, 4 * LANES), BF16),
            pltpu.VMEM((2, FACE_ROWS, 2 * LANES), BF16),
            pltpu.VMEM((2, FACE_ROWS, 4 * LANES), BF16),
            pltpu.VMEM((2, DEEP * LAYER, LANES), F32),
            pltpu.VMEM((5, 8 * LAYER, SOURCES), BF16),
            pltpu.VMEM((12 * LANES, LANES), BF16),
            pltpu.VMEM((ITERS + 1, 2 * G, LANES), F32),
            pltpu.VMEM((ALL, LANES), F32),
            pltpu.VMEM((ALL, LANES), F32),
            pltpu.VMEM((ALL, LANES), F32),
            pltpu.VMEM((128, PLANE * G), BF16),
            pltpu.VMEM((32, 128), F32),
            pltpu.VMEM((3, 4, 128), F32),
            pltpu.VMEM((3, PLANE - 1, 4, 128), F32),
            pltpu.VMEM((3, 4, 128), F32),
            pltpu.VMEM((3, ZLINE - 1, 4, 128), F32),
            pltpu.SemaphoreType.DMA((ITERS, 6)),
            pltpu.SemaphoreType.DMA((ITERS, 6)),
            pltpu.SemaphoreType.DMA((4,)),
            pltpu.SemaphoreType.DMA((4,)),
            pltpu.SemaphoreType.DMA((3,)),
            pltpu.SemaphoreType.DMA((3,)),
            pltpu.SemaphoreType.DMA((3,)),
            pltpu.SemaphoreType.DMA((3,)),
        ],
        compiler_params=pltpu.CompilerParams(
            collective_id=0, has_side_effects=True, vmem_limit_bytes=60 << 20
        ),
        name="sweeps",
    )(
        body_load,
        probe_load,
        density,
        jnp.transpose(link_types, (0, 3, 1, 2)),
        off_blocks,
        self_blocks,
        block_owner,
    )
    return state, adjoint, coarse.reshape(GPB)


def solution(mesh):
    in_specs = (
        P("gx", "gy", "gz", None),
        P("gx", "gy", "gz", None),
        P("gx", "gy", "gz"),
        P("gx", "gy", "gz", None),
        P(),
        P(),
        P("gx", "gy", "gz"),
    )
    out_specs = (P("gx", "gy", "gz", None), P("gx", "gy", "gz", None), P(("gx", "gy", "gz")))
    return jax.shard_map(local, mesh=mesh, in_specs=in_specs, out_specs=out_specs, check_vma=False)
```

```python
import functools

import jax
import jax.numpy as jnp
from jax import lax
from jax.experimental import pallas as pl
from jax.experimental.pallas import tpu as pltpu
from jax.sharding import PartitionSpec as P

MESH = pl.DeviceIdType.MESH
F32, BF16 = jnp.float32, jnp.bfloat16
ITERS = 4
GPB = 8
NX, NY, NZ = 2, 4, 8
G = NX * NY * NZ
DOF, LANES = 192, 256
LAYER, DEEP = NY * NZ, 3
ALL = G + DEEP * LAYER
UPX, LOWX, LOWY, UPY, LOWZ, UPZ, ROWS = 64, 192, 224, 272, 320, 352, 384
FACES = (0, 48, 96, 128)
FACE_ROWS = 160
OUT, SOURCES = 96, 256
SX, SY, SZ, CY = 16, 4, 8, 8
PLANE, ZLINE = 32, 16
LOCAL_GAIN = (3 / 2.125) ** 0.5
NT_DIMS = (((1,), (1,)), ((), ()))


def iota(shape, dim):
    return lax.broadcasted_iota(jnp.int32, shape, dim)


def total(values):
    values = list(values)
    while len(values) > 1:
        pairs = [values[i] + values[i + 1] for i in range(0, len(values) - 1, 2)]
        values = pairs + values[len(pairs) * 2 :]
    return values[0]


def place(i, j):
    i, j = min(i, j), max(i, j)
    return i * 5 - i * (i - 1) // 2 + (j - i)


def entries(row, size):
    lane = iota(row.shape, 1)
    table = {}
    for i in range(size):
        for j in range(i, size):
            table[i, j] = table[j, i] = jnp.sum(
                jnp.where(lane == place(i, j), row, 0.0), axis=1, keepdims=True
            )
    return table


def bilinear(left, table, right):
    return total(
        left[i] * total(table[i, j] * right[j] for j in right) for i in left
    )


def sweeps(table, count, image):
    one = jnp.ones_like(table[0, 0])
    residual, answer, steps = {0: one}, {}, []
    for _ in range(count):
        moved = image(residual)
        projected = bilinear(residual, table, moved)
        energy = bilinear(moved, table, moved)
        step = projected / (energy + 1e-6)
        steps.append(step)
        for i, c in residual.items():
            answer[i] = answer[i] + step * c if i in answer else step * c
        for i, c in moved.items():
            residual[i] = residual[i] - step * c if i in residual else -(step * c)
    return steps, answer, residual


def kernel(body, probe, dens, links, offb, selfb, owner, state_out, adjoint_out, coarse_out,
           x_one, x_two, faces_one, faces_two, vg, pick, table, v, su, sc, rp, hot, rr, mp, mps, mz, mzs, mq, mqs, split, tile, tiles,
           hs, hr, fs, fr, ps, pr, zs, zr):
    gx, gy, gz = lax.axis_index("gx"), lax.axis_index("gy"), lax.axis_index("gz")
    zh, yc = gx // CY, gx % CY
    me_p = yc * SY + gy
    me_z = zh * SZ + gz
    ghost = jnp.logical_or(gx == CY - 1, gx == CY)
    behind = jnp.logical_or(gx == CY - 2, gx == CY + 1)
    mirror = (gx == CY).astype(jnp.int32)
    across_peer = (2 * CY - 1 - gx, gy, gz)
    behind_peer = (jnp.where(gx == CY + 1, CY - 1, CY), gy, gz)
    greeter = (jnp.where(gx == CY, CY - 2, CY + 1), gy, gz)

    def plane_peer(i):
        p = (me_p + 1 + i) % PLANE
        return (zh * CY + p // SY, p % SY, gz)

    def line_peer(i):
        q = (me_z + 1 + i) % ZLINE
        return (q // SZ * CY + yc, gy, q % SZ)

    barrier = pltpu.get_barrier_semaphore()

    def greet_plane(i, _):
        pl.semaphore_signal(barrier, inc=1, device_id=plane_peer(i), device_id_type=MESH)
        return 0

    def greet_line(i, _):
        pl.semaphore_signal(barrier, inc=1, device_id=line_peer(i), device_id_type=MESH)
        return 0

    lax.fori_loop(0, ZLINE - 1, greet_line, 0)

    @pl.when(ghost)
    def _():
        for peer in (across_peer, greeter):
            pl.semaphore_signal(barrier, inc=1, device_id=peer, device_id_type=MESH)

    @pl.when(behind)
    def _():
        pl.semaphore_signal(barrier, inc=1, device_id=behind_peer, device_id_type=MESH)

    lax.fori_loop(0, PLANE - 1, greet_plane, 0)

    sends = (
        ((gx < SX - 1) & (gx != CY - 1), (gx + 1, gy, gz)),
        ((gx > 0) & (gx != CY), (gx - 1, gy, gz)),
        (gy < SY - 1, (gx, gy + 1, gz)),
        (gy > 0, (gx, gy - 1, gz)),
        (gz < SZ - 1, (gx, gy, gz + 1)),
        (gz > 0, (gx, gy, gz - 1)),
    )
    comes = (
        (gx > 0) & (gx != CY),
        (gx < SX - 1) & (gx != CY - 1),
        gy > 0,
        gy < SY - 1,
        gz > 0,
        gz < SZ - 1,
    )
    lands = (LOWX, jnp.where(gx == CY + 1, LOWX, UPX), LOWY, UPY, LOWZ, UPZ)
    deep_rows = {0: (48, 32), 1: (32, 16), 2: (32, 16), 3: (16, 16)}

    def rows_of(k, d, deep):
        return deep_rows[k][(d - 2) // 2] if deep else 16

    def halo(k, d, deep=False):
        x = x_one.at[k] if k < 2 else x_two.at[k - 2]
        faces = faces_one.at[k] if k < 2 else faces_two.at[k - 2]
        if d < 2:
            at = jnp.where(gx == CY, 0, LAYER) if d == 0 else 0
            src = x.at[pl.ds(pl.multiple_of(at, LAYER), LAYER)]
            dst = x.at[pl.ds(pl.multiple_of(lands[d], LAYER), LAYER)]
        else:
            size = rows_of(k, d, deep)
            src = faces.at[pl.ds(FACES[d - 2], size)]
            dst = x.at[pl.ds(lands[d], size)]
        return pltpu.make_async_remote_copy(
            src_ref=src,
            dst_ref=dst,
            send_sem=hs.at[k, d],
            recv_sem=hr.at[k, d],
            device_id=sends[d][1],
            device_id_type=MESH,
        )

    def for_halos(k, ways, conditions, act):
        for d in ways:
            if d < 2:
                @pl.when(conditions[d])
                def _():
                    act(halo(k, d))
            else:
                @pl.when(conditions[d] & ghost)
                def _():
                    act(halo(k, d, True))

                @pl.when(conditions[d] & jnp.logical_not(ghost))
                def _():
                    act(halo(k, d, False))

    def start_halos(k, ways=range(6)):
        for_halos(k, ways, [c for c, _ in sends], lambda copy: copy.start())

    def wait_halos(k, ways=range(6)):
        for_halos(k, ways, comes, lambda copy: copy.wait_recv())

    def far_copy(m):
        first = jnp.where(gx == CY + 1, 0, LAYER)
        at = (LAYER, 0, first, LAYER - first)[m]
        return pltpu.make_async_remote_copy(
            src_ref=x_one.at[0, pl.ds(pl.multiple_of(at, LAYER), LAYER)],
            dst_ref=x_one.at[0, pl.ds(UPX + m * LAYER, LAYER)],
            send_sem=fs.at[m],
            recv_sem=fr.at[m],
            device_id=across_peer if m < 2 else behind_peer,
            device_id_type=MESH,
        )

    def clear(at, size, first=True):
        for k in range(0 if first else 1, 2):
            x_one[k, pl.ds(at, size), :] = jnp.zeros((size, 2 * LANES), BF16)
        x_two[:, pl.ds(at, size), :] = jnp.zeros((2, size, 4 * LANES), BF16)

    clear(UPX + LAYER, 3 * LAYER, False)

    @pl.when(jnp.logical_not(ghost))
    def _():
        x_one[0, pl.ds(UPX + LAYER, 3 * LAYER), :] = jnp.zeros((3 * LAYER, 2 * LANES), BF16)
        for at, size in ((LOWY, 48), (UPY, 48), (LOWZ, 32), (UPZ, 32)):
            clear(at + 16, size - 16)

    @pl.when(ghost)
    def _():
        for k in range(1, ITERS):
            for d in range(2, 6):
                size, full = deep_rows[k][(d - 2) // 2], deep_rows[0][(d - 2) // 2]
                if size < full:
                    rest = pl.ds(lands[d] + size, full - size)
                    if k < 2:
                        x_one[k, rest, :] = jnp.zeros((full - size, 2 * LANES), BF16)
                    else:
                        x_two[k - 2, rest, :] = jnp.zeros((full - size, 4 * LANES), BF16)

    for absent, at, size in (
        (gx == 0, LOWX, LAYER),
        (gx == SX - 1, UPX, LAYER),
        (gy == 0, LOWY, 48),
        (gy == SY - 1, UPY, 48),
        (gz == 0, LOWZ, 32),
        (gz == SZ - 1, UPZ, 32),
    ):
        @pl.when(absent)
        def _():
            clear(at, size)

    own = (mirror, 1 - mirror)

    eye8 = iota((8, 8), 0) == iota((8, 8), 1)

    def column(row_of):
        return jnp.concatenate(
            [
                jnp.sum(
                    jnp.where(eye8, jnp.broadcast_to(row_of(own[a], b).astype(F32), (8, 8)), 0.0),
                    axis=1,
                    keepdims=True,
                )
                for a in range(NX)
                for b in range(NY)
            ],
            axis=0,
        )

    kinds = [column(lambda a, b: links[a, k, b : b + 1, :]) for k in range(7)]
    density = column(lambda a, b: dens[a, b : b + 1, :])
    owners = column(lambda a, b: owner[a, b : b + 1, :])

    eye = iota((DOF, DOF), 0) == iota((DOF, DOF), 1)
    eye_low = jnp.where(eye, 1.0, 0.0).astype(BF16)
    diagonals = []
    table[...] = jnp.zeros(table.shape, BF16)
    for t in range(4):
        block = selfb[t]
        diagonals.append(
            jnp.sum(jnp.where(eye, block.astype(F32), 0.0), axis=0, keepdims=True)
        )
        upper = lax.dot_general(eye_low, offb[t], NT_DIMS, preferred_element_type=F32)
        table[pl.ds(t * LANES, DOF), pl.ds(0, DOF)] = upper.astype(BF16)
        table[pl.ds((4 + t) * LANES, DOF), pl.ds(0, DOF)] = offb[t]
        table[pl.ds((8 + t) * LANES, DOF), pl.ds(0, DOF)] = block

    def prepare(at, size, kinds, density):
        scale = density * jnp.sqrt(density)
        pivots = jnp.ones((size, DOF), F32)
        for t in range(4):
            pivots = jnp.where(kinds[6] == float(t), diagonals[t], pivots)
        rows = pl.ds(at, size)
        rp[rows, :] = jnp.ones((size, LANES), F32)
        rp[rows, pl.ds(0, DOF)] = 1.0 / pivots
        sc[rows, :] = jnp.broadcast_to(scale, (size, LANES))
        su[rows, :] = rp[rows, :] * sc[rows, :]
        g = iota((size, 1), 0) + at
        gl, here, gyy, gzz = g // LAYER, g % LAYER, g // NZ % NY, g % NZ
        on, back = here + 2 * LAYER, here
        y, z = OUT + gl * NZ + gzz, OUT + gl * NY + gyy
        sources = (
            jnp.where(mirror == 1, back, on),
            jnp.where(gyy < NY - 1, here + LAYER + 8, y + FACES[1]),
            jnp.where(gzz < NZ - 1, here + LAYER + 1, z + FACES[3]),
            jnp.where(mirror == 1, on, back),
            jnp.where(gyy > 0, here + LAYER - 8, y + FACES[0]),
            jnp.where(gzz > 0, here + LAYER - 1, z + FACES[2]),
        )
        across = iota((size, SOURCES), 1).astype(F32)
        sources = [a.astype(F32) for a in sources]
        for side in range(2):
            for t in range(4):
                chosen = jnp.zeros((size, SOURCES), F32)
                for k in range(3 * side, 3 * side + 3):
                    code = jnp.where(kinds[k] == float(t), sources[k], -1.0)
                    chosen = jnp.where(across == code, 1.0, chosen)
                chosen = chosen.astype(BF16)
                for i in range(size // LAYER):
                    pick[at // LAYER + i, pl.ds((4 * side + t) * LAYER, LAYER), :] = chosen[
                        i * LAYER : (i + 1) * LAYER
                    ]

    prepare(0, G, kinds, density)

    v[0] = jnp.zeros((2 * G, LANES), F32)
    for a in range(NX):
        for f, load in enumerate((body, probe)):
            v[0, pl.ds(f * G + a * LAYER, LAYER), pl.ds(0, DOF)] = load[own[a]].reshape(LAYER, DOF)

    r = iota((FACE_ROWS, 1), 0)
    along_y, along_z = r % 48, r % 32
    face_y = along_y // 8 * LAYER + along_y % 8
    face_z = along_z // 4 * LAYER + along_z % 4 * 8
    face = jnp.where(
        r < 48, face_y + 24, jnp.where(r < 96, face_y, jnp.where(r < 128, face_z + 7, face_z))
    )
    outer = jnp.where(iota((FACE_ROWS, ALL), 1) == face, 1.0, 0.0).astype(BF16)

    def both(a):
        return jnp.concatenate([a, a], axis=0)

    def scaled(field, factor, parts):
        size = factor.shape[0]
        u = field * both(factor)
        high = u.astype(BF16)
        out = [high[:size], high[size:]]
        if parts == 2:
            low = (u - high.astype(F32)).astype(BF16)
            out += [low[:size], low[size:]]
        return out

    def fold(a, size):
        return a[: 2 * size] + a[2 * size :] if a.shape[0] == 4 * size else a

    def straight(parts, kind):
        size = kind.shape[0]
        masks = [jnp.broadcast_to(kind == float(t), (size, LANES)) for t in range(4)]
        left = []
        for part in parts:
            part = part.astype(F32)
            left.append(
                jnp.concatenate([jnp.where(m, part, 0.0).astype(BF16) for m in masks], axis=1)
            )
        left = jnp.concatenate(left, axis=0)
        return fold(
            jnp.dot(left, table[pl.ds(8 * LANES, 4 * LANES)], preferred_element_type=F32), size
        )

    def coupled(sources):
        size = len(sources) * LAYER
        highs, lows = ([], []), ([], [])
        for i, source in enumerate(sources):
            z = jnp.dot(pick[i], source, preferred_element_type=F32)
            if z.shape[1] == 4 * LANES:
                z = z[:, : 2 * LANES] + z[:, 2 * LANES :]
            high = z.astype(BF16)
            low = (z - high.astype(F32)).astype(BF16)
            for f in range(2):
                for a, out in ((high, highs), (low, lows)):
                    out[f].append(
                        jnp.concatenate(
                            [
                                a[t * LAYER : (t + 1) * LAYER, f * LANES : (f + 1) * LANES]
                                for t in range(8)
                            ],
                            axis=1,
                        )
                    )
        left = jnp.concatenate(highs[0] + highs[1] + lows[0] + lows[1], axis=0)
        return fold(jnp.dot(left, table[pl.ds(0, 8 * LANES)], preferred_element_type=F32), size)

    def sources_of(k, layers):
        def rows(at, size):
            return x_one[k, pl.ds(at, size), :] if k < 2 else x_two[k - 2, pl.ds(at, size), :]

        outside = rows(LOWY, FACE_ROWS)
        out = []
        for i in range(layers):
            near = (
                [rows(LOWX, LAYER), rows(0, 2 * LAYER)]
                if i == 0
                else [rows((i - 1) * LAYER, 3 * LAYER)]
            )
            out.append(jnp.concatenate(near + [outside], axis=0))
        return out

    def faces_of(sent):
        return jnp.dot(
            outer[:, : sent.shape[0]], sent, preferred_element_type=F32
        ).astype(BF16)

    def ship(k):
        more = (ITERS - k) * LAYER
        own_parts = scaled(v[k], su[pl.ds(0, G), :], 1 if k < 2 else 2)
        far_parts = scaled(
            jnp.concatenate([vg[f, pl.ds(0, more), :] for f in range(2)], axis=0),
            su[pl.ds(G, more), :],
            1 if k < 2 else 2,
        )
        sent = jnp.concatenate(own_parts, axis=1)
        beyond = jnp.concatenate(far_parts, axis=1)
        x, i = (x_one, k) if k < 2 else (x_two, k - 2)
        x[i, pl.ds(0, G), :] = sent

        @pl.when(ghost)
        def _():
            x[i, pl.ds(UPX, more), :] = beyond

        (faces_one if k < 2 else faces_two)[i] = faces_of(
            jnp.concatenate([sent, beyond], axis=0)
        )
        last = more - LAYER
        return [
            jnp.concatenate([a, b[:last]], axis=0) if last else a
            for a, b in zip(own_parts, far_parts)
        ]

    def gram(fields, i, j):
        product = fields[i] * fields[j]
        for f in range(2):
            part = jnp.sum(product[f * G : (f + 1) * G], axis=0, keepdims=True)
            rr[pl.ds(f * 16 + place(i, j), 1), :] = part[:, :128] + part[:, 128:]

    def gram_rows():
        sums = jnp.sum(rr[...], axis=1, keepdims=True)
        spot = iota((16, 128), 0) == iota((16, 128), 1)
        return [
            jnp.sum(jnp.where(spot, sums[f * 16 : f * 16 + 16], 0.0), axis=0, keepdims=True)
            for f in range(2)
        ]

    def start_plane(e):
        def one(i, _):
            if e == 0:
                src, dst = mp, mps.at[PLANE - 2 - i]
            else:
                src, dst = mq, mqs.at[PLANE - 2 - i]
            pltpu.make_async_remote_copy(
                src_ref=src, dst_ref=dst, send_sem=ps.at[e], recv_sem=pr.at[e],
                device_id=plane_peer(i), device_id_type=MESH,
            ).start()
            return 0

        lax.fori_loop(0, PLANE - 1, one, 0)

    def start_line(e):
        for o in sorted(range(1, ZLINE), key=lambda o: -min(o, ZLINE - o)):
            i = o - 1
            if e == 0:
                src, dst = mz, mzs.at[ZLINE - 2 - i]
            else:
                src, dst = tile.at[(me_z + o) % ZLINE], tiles.at[ZLINE - 2 - i]
            pltpu.make_async_remote_copy(
                src_ref=src, dst_ref=dst, send_sem=zs.at[e], recv_sem=zr.at[e],
                device_id=line_peer(i), device_id_type=MESH,
            ).start()

    def wait_all(buffer, sem):
        pltpu.make_async_copy(buffer, buffer, sem).wait()

    rr[...] = jnp.zeros(rr.shape, F32)
    sent = scaled(v[0], su[pl.ds(0, G), :], 1)

    def split3(a):
        first = a.astype(BF16).astype(F32)
        second = (a - first).astype(BF16).astype(F32)
        return [first, second, a - first - second]

    lane = iota((G, LANES), 1)
    notes = sent[0].astype(F32)
    for i, col in enumerate(kinds + split3(density)):
        notes = jnp.where(lane == DOF + i, col, notes)
    sent = jnp.concatenate([notes.astype(BF16), sent[1]], axis=1)
    x_one[0, pl.ds(0, G), :] = sent

    @pl.when(jnp.logical_not(ghost))
    def _():
        faces_one[0] = faces_of(sent)


    inner = [v[0]]
    for _ in range(ITERS - 1):
        parts = scaled(inner[-1], su[pl.ds(0, G), :], 1)
        near = jnp.concatenate(parts, axis=1)

        def empty(size):
            return jnp.zeros((size, 2 * LANES), BF16)

        moved = LOCAL_GAIN * coupled(
            [
                jnp.concatenate([empty(LAYER), near, empty(FACE_ROWS)], axis=0),
                jnp.concatenate([near, empty(LAYER + FACE_ROWS)], axis=0),
            ]
        )
        inner.append((moved + straight(parts, kinds[6])) * both(sc[pl.ds(0, G), :]))
    for i in range(ITERS):
        for j in range(i, ITERS):
            gram(inner, i, j)

    spread = iota((G, 128), 1) == iota((G, 128), 0)

    def as_row(col):
        return jnp.sum(jnp.where(spread, col, 0.0), axis=0, keepdims=True)

    rows = gram_rows()
    mp[0:1, :] = rows[0]
    mp[1:2, :] = rows[1]
    mp[2:3, :] = as_row(owners)
    mp[3:4, :] = as_row(density)

    extra = 2 * ghost.astype(jnp.int32) + behind.astype(jnp.int32)
    pl.semaphore_wait(barrier, PLANE - 1 + ZLINE - 1 + extra)

    @pl.when(ghost)
    def _():
        for m in range(2):
            far_copy(m).start()

    @pl.when(behind)
    def _():
        for m in range(2, 4):
            far_copy(m).start()

    start_halos(0, (0, 1))

    @pl.when(jnp.logical_not(ghost))
    def _():
        for d in range(2, 6):
            @pl.when(sends[d][0])
            def _():
                halo(0, d).start()

    start_plane(0)
    wait_all(mps, pr.at[0])
    mz[...] = mp[...] + total(mps[i] for i in range(PLANE - 1))
    start_line(0)

    low_half = iota((1, 128), 1) < G

    def joined(a, b):
        return jnp.where(low_half, a, pltpu.roll(b, G, 1))

    def gathered(row):
        parts = [mps[i, row : row + 1, :] for i in range(PLANE - 1)]
        parts.append(mp[row : row + 1, :])
        return [joined(parts[2 * m], parts[2 * m + 1]) for m in range(PLANE // 2)]

    q = iota((128, 1), 0)
    bins = (((q // 64 * CY + yc) * SY + gy) * SZ + q // 8 % 8) * GPB + q % 8
    bins = bins.astype(F32)
    for m, row in enumerate(gathered(2)):
        hot[:, pl.ds(m * 128, 128)] = jnp.where(row == bins, 1.0, 0.0).astype(BF16)

    masses = gathered(3)
    split[pl.ds(96, 32), :] = jnp.zeros((32, PLANE * G), BF16)

    wait_halos(0, (0, 1))

    @pl.when(ghost)
    def _():
        for m in range(4):
            far_copy(m).wait_recv()
        faces_one[0] = faces_of(x_one[0, pl.ds(0, ALL), :])
        for d in range(2, 6):
            @pl.when(sends[d][0])
            def _():
                halo(0, d, True).start()

    notes = x_one[0, pl.ds(UPX, DEEP * LAYER), pl.ds(128, 128)].astype(F32)
    notes = [notes[:, DOF - 128 + i : DOF - 127 + i] for i in range(10)]
    prepare(G, DEEP * LAYER, notes[:7], notes[7] + notes[8] + notes[9])
    kind = jnp.concatenate([kinds[6], notes[6]], axis=0)
    beyond = su[pl.ds(G, DEEP * LAYER), :]
    beyond = jnp.where(beyond > 0.0, 1.0 / beyond, 0.0)
    parts = []
    for f in range(2):
        parts.append(x_one[0, pl.ds(0, ALL), pl.ds(f * LANES, LANES)])
        vg[f] = parts[f][G:].astype(F32) * beyond

    spots = {}
    for i in range(ITERS + 1):
        for j in range(ITERS + 1):
            if i + j < 2 * ITERS:
                spots[i, j] = len(spots) % 12 + 16 * (len(spots) // 12)
    lane = iota((G, 128), 1)
    columns = [jnp.zeros((G, 128), F32)]

    def products(i, j):
        part = v[i, pl.ds(G, G), :] * rp[pl.ds(0, G), :] * v[j, pl.ds(0, G), :]
        col = jnp.sum(part, axis=1, keepdims=True)
        columns[0] = jnp.where(lane == spots[i, j], col, columns[0])

    guess = None
    for k in range(ITERS):
        size = ALL - k * LAYER
        alone = straight(parts, kind[:size])
        wait_halos(k, range(2, 6) if k == 0 else range(6))
        moved = (coupled(sources_of(k, size // LAYER)) + alone) * both(sc[pl.ds(0, size), :])
        ours = jnp.concatenate([moved[:G], moved[size : size + G]], axis=0)
        if k == 0:
            wait_all(mzs, zr.at[0])
            row = mz[0:2, :] + total(mzs[i, 0:2, :] for i in range(ZLINE - 1))
            guess, _, _ = sweeps(
                entries(row, ITERS), ITERS - 1, lambda c: {i + 1: e for i, e in c.items()}
            )
            guess = [jnp.where((s > 1e-3) & (s < 1e6), s, 1.0) for s in guess]
        if k < ITERS - 1:
            step = jnp.concatenate(
                [jnp.broadcast_to(guess[k][f : f + 1], (G, 1)) for f in range(2)], axis=0
            )
            v[k + 1] = v[k] - step * ours
            for f in range(2):
                more = size - G
                vg[f, pl.ds(0, more), :] = (
                    vg[f, pl.ds(0, more), :]
                    - guess[k][f : f + 1] * moved[f * size + G : (f + 1) * size]
                )
            parts = ship(k + 1)
            start_halos(k + 1)
        else:
            v[k + 1] = ours
        for i in range(k + 2):
            gram(v, i, k + 1)
        if k == 0:
            gram(v, 0, 0)
            products(0, 0)
        for i in range(k + 1):
            products(i, k + 1)
            products(k + 1, i)
        if 0 < k + 1 < ITERS:
            products(k + 1, k + 1)

    rows = gram_rows()
    turned = jnp.transpose(jnp.concatenate([columns[0], jnp.zeros((G, 128), F32)], axis=0))
    mq[...] = jnp.where(low_half, turned[0:16], pltpu.roll(turned[16:32], G, 1))
    mq[12:13, :] = rows[0]
    mq[13:14, :] = rows[1]
    start_plane(1)
    wait_all(mqs, pr.at[1])
    sums = mq[12:14, :] + total(mqs[i, 12:14, :] for i in range(PLANE - 1))
    sub = iota((16, 128), 0)
    for m in range(PLANE // 2):
        a = mqs[2 * m]
        b = mqs[2 * m + 1] if 2 * m + 1 < PLANE - 1 else mq[...]
        low = jnp.where(low_half, a, pltpu.roll(b, G, 1))
        high = jnp.where(low_half, pltpu.roll(a, G, 1), b)
        low = jnp.where(sub < 12, low, jnp.where(sub == 12, masses[m], 0.0))
        high = jnp.where(sub < 12, high, 0.0)
        for i, part in enumerate(split3(jnp.concatenate([low, high], axis=0))):
            split[pl.ds(i * 32, 32), pl.ds(m * 128, 128)] = part.astype(BF16)
    blocks = lax.dot_general(hot[...], split[...], NT_DIMS, preferred_element_type=F32)
    blocks = blocks + pltpu.roll(blocks, 96, 1) + pltpu.roll(blocks, 64, 1)
    lane = iota((8, 128), 1)
    first = iota((8, 128), 0) == 0
    shared = jnp.where(
        first & (lane >= 32) & (lane < 48),
        pltpu.roll(sums, 32, 1)[0:1],
        jnp.where(first & (lane >= 48) & (lane < 64), pltpu.roll(sums, 48, 1)[1:2], 0.0),
    )
    for i in range(ZLINE):
        tile[i] = jnp.where(lane < 32, blocks[i * 8 : (i + 1) * 8], shared)
    start_line(1)
    wait_all(tiles, zr.at[1])
    mine = tile[me_z] + total(tiles[i] for i in range(ZLINE - 1))
    row = jnp.concatenate(
        [pltpu.roll(mine, 96, 1)[0:1], pltpu.roll(mine, 80, 1)[0:1]], axis=0
    )

    inverse = [1.0 / s for s in guess]

    def newton(c):
        out = {}
        for i, e in c.items():
            if i < ITERS - 1:
                part = e * inverse[i]
                out[i] = out[i] + part if i in out else part
                out[i + 1] = out[i + 1] - part if i + 1 in out else -part
            else:
                out[i + 1] = e
        return out

    _, answer, left = sweeps(entries(row, ITERS + 1), ITERS, newton)

    def combine(coefficients, f):
        return total(
            c[f : f + 1, :] * v[i, pl.ds(f * G, G), :] for i, c in coefficients.items()
        )

    solved = [combine(answer, f) * rp[pl.ds(0, G), :] for f in range(2)]
    for a in range(NX):
        for f, out in enumerate((state_out, adjoint_out)):
            out[own[a]] = solved[f][a * LAYER : (a + 1) * LAYER, :DOF].reshape(NY, NZ, DOF)
    applied = {i: (1.0 - c if i == 0 else -c) for i, c in left.items()}
    lane = iota((1, 128), 1)
    weights = jnp.zeros((1, 128), F32)
    for (i, j), spot in spots.items():
        terms = []
        if i < ITERS:
            terms.append(answer[i][1:2] * applied[j][0:1])
        if j < ITERS:
            terms.append(answer[j][0:1] * applied[i][1:2])
        weights = jnp.where(lane == spot, total(terms), weights)
    above = -1.5 * jnp.sum(mine * weights, axis=1, keepdims=True)
    below = mine[:, 12:13]
    ratio = jnp.where(below > 0.0, above / below, 0.0)
    coarse_out[...] = jnp.sum(jnp.where(eye8, ratio, 0.0), axis=0, keepdims=True)

    for k in range(ITERS):
        for_halos(k, range(6), [c for c, _ in sends], lambda copy: copy.wait_send())

    @pl.when(ghost)
    def _():
        for m in range(2):
            far_copy(m).wait_send()

    @pl.when(behind)
    def _():
        for m in range(2, 4):
            far_copy(m).wait_send()

    for buffer, sem in ((mps, ps.at[0]), (mqs, ps.at[1]), (mzs, zs.at[0]), (tiles, zs.at[1])):
        wait_all(buffer, sem)


def local(body_load, probe_load, density, link_types, off_blocks, self_blocks, block_owner):
    vmem = pl.BlockSpec(memory_space=pltpu.VMEM)
    state, adjoint, coarse = pl.pallas_call(
        kernel,
        out_shape=(
            jax.ShapeDtypeStruct(body_load.shape, F32),
            jax.ShapeDtypeStruct(body_load.shape, F32),
            jax.ShapeDtypeStruct((1, GPB), F32),
        ),
        in_specs=[vmem] * 7,
        out_specs=(vmem,) * 3,
        scratch_shapes=[
            pltpu.VMEM((2, ROWS, 2 * LANES), BF16),
            pltpu.VMEM((2, ROWS, 4 * LANES), BF16),
            pltpu.VMEM((2, FACE_ROWS, 2 * LANES), BF16),
            pltpu.VMEM((2, FACE_ROWS, 4 * LANES), BF16),
            pltpu.VMEM((2, DEEP * LAYER, LANES), F32),
            pltpu.VMEM((5, 8 * LAYER, SOURCES), BF16),
            pltpu.VMEM((12 * LANES, LANES), BF16),
            pltpu.VMEM((ITERS + 1, 2 * G, LANES), F32),
            pltpu.VMEM((ALL, LANES), F32),
            pltpu.VMEM((ALL, LANES), F32),
            pltpu.VMEM((ALL, LANES), F32),
            pltpu.VMEM((128, PLANE * G), BF16),
            pltpu.VMEM((32, 128), F32),
            pltpu.VMEM((4, 128), F32),
            pltpu.VMEM((PLANE - 1, 4, 128), F32),
            pltpu.VMEM((4, 128), F32),
            pltpu.VMEM((ZLINE - 1, 4, 128), F32),
            pltpu.VMEM((16, 128), F32),
            pltpu.VMEM((PLANE - 1, 16, 128), F32),
            pltpu.VMEM((128, PLANE * G), BF16),
            pltpu.VMEM((ZLINE, 8, 128), F32),
            pltpu.VMEM((ZLINE - 1, 8, 128), F32),
            pltpu.SemaphoreType.DMA((ITERS, 6)),
            pltpu.SemaphoreType.DMA((ITERS, 6)),
            pltpu.SemaphoreType.DMA((4,)),
            pltpu.SemaphoreType.DMA((4,)),
            pltpu.SemaphoreType.DMA((2,)),
            pltpu.SemaphoreType.DMA((2,)),
            pltpu.SemaphoreType.DMA((2,)),
            pltpu.SemaphoreType.DMA((2,)),
        ],
        compiler_params=pltpu.CompilerParams(
            collective_id=0, has_side_effects=True, vmem_limit_bytes=60 << 20
        ),
        name="sweeps",
    )(
        body_load,
        probe_load,
        density,
        jnp.transpose(link_types, (0, 3, 1, 2)),
        off_blocks,
        self_blocks,
        block_owner,
    )
    return state, adjoint, coarse.reshape(GPB)


def solution(mesh):
    in_specs = (
        P("gx", "gy", "gz", None),
        P("gx", "gy", "gz", None),
        P("gx", "gy", "gz"),
        P("gx", "gy", "gz", None),
        P(),
        P(),
        P("gx", "gy", "gz"),
    )
    out_specs = (P("gx", "gy", "gz", None), P("gx", "gy", "gz", None), P(("gx", "gy", "gz")))
    return jax.shard_map(local, mesh=mesh, in_specs=in_specs, out_specs=out_specs, check_vma=False)
```

```python
import functools

import jax
import jax.numpy as jnp
from jax import lax
from jax.experimental import pallas as pl
from jax.experimental.pallas import tpu as pltpu
from jax.sharding import PartitionSpec as P

MESH = pl.DeviceIdType.MESH
F32, BF16 = jnp.float32, jnp.bfloat16
ITERS = 4
GPB = 8
NX, NY, NZ = 2, 4, 8
G = NX * NY * NZ
DOF, LANES = 192, 256
LAYER, DEEP = NY * NZ, 3
ALL = G + DEEP * LAYER
UPX, LOWX, LOWY, UPY, LOWZ, UPZ, ROWS = 64, 192, 224, 272, 320, 352, 384
FACES = (0, 48, 96, 128)
FACE_ROWS = 160
OUT, SOURCES = 96, 256
SX, SY, SZ, CY = 16, 4, 8, 8
PLANE, ZLINE = 32, 16
LOCAL_GAIN = (3 / 2.125) ** 0.5
NT_DIMS = (((1,), (1,)), ((), ()))


def iota(shape, dim):
    return lax.broadcasted_iota(jnp.int32, shape, dim)


def total(values):
    values = list(values)
    while len(values) > 1:
        pairs = [values[i] + values[i + 1] for i in range(0, len(values) - 1, 2)]
        values = pairs + values[len(pairs) * 2 :]
    return values[0]


def place(i, j):
    i, j = min(i, j), max(i, j)
    return i * 5 - i * (i - 1) // 2 + (j - i)


def entries(row, size):
    lane = iota(row.shape, 1)
    table = {}
    for i in range(size):
        for j in range(i, size):
            table[i, j] = table[j, i] = jnp.sum(
                jnp.where(lane == place(i, j), row, 0.0), axis=1, keepdims=True
            )
    return table


def bilinear(left, table, right):
    return total(
        left[i] * total(table[i, j] * right[j] for j in right) for i in left
    )


def sweeps(table, count, image):
    one = jnp.ones_like(table[0, 0])
    residual, answer, steps = {0: one}, {}, []
    for _ in range(count):
        moved = image(residual)
        projected = bilinear(residual, table, moved)
        energy = bilinear(moved, table, moved)
        step = projected / (energy + 1e-6)
        steps.append(step)
        for i, c in residual.items():
            answer[i] = answer[i] + step * c if i in answer else step * c
        for i, c in moved.items():
            residual[i] = residual[i] - step * c if i in residual else -(step * c)
    return steps, answer, residual


def kernel(body, probe, dens, links, offb, selfb, owner, state_out, adjoint_out, coarse_out,
           x_one, x_two, faces_one, faces_two, vg, pick, table, v, su, sc, rp, hot, rr, mp, mps, mz, mzs, mq, mqs, me, mes, split, tile, tiles,
           hs, hr, fs, fr, ps, pr, zs, zr):
    gx, gy, gz = lax.axis_index("gx"), lax.axis_index("gy"), lax.axis_index("gz")
    zh, yc = gx // CY, gx % CY
    me_p = yc * SY + gy
    me_z = zh * SZ + gz
    ghost = jnp.logical_or(gx == CY - 1, gx == CY)
    behind = jnp.logical_or(gx == CY - 2, gx == CY + 1)
    mirror = (gx == CY).astype(jnp.int32)
    across_peer = (2 * CY - 1 - gx, gy, gz)
    behind_peer = (jnp.where(gx == CY + 1, CY - 1, CY), gy, gz)
    greeter = (jnp.where(gx == CY, CY - 2, CY + 1), gy, gz)

    def plane_peer(i):
        p = (me_p + 1 + i) % PLANE
        return (zh * CY + p // SY, p % SY, gz)

    def line_peer(i):
        q = (me_z + 1 + i) % ZLINE
        return (q // SZ * CY + yc, gy, q % SZ)

    barrier = pltpu.get_barrier_semaphore()

    def greet_plane(i, _):
        pl.semaphore_signal(barrier, inc=1, device_id=plane_peer(i), device_id_type=MESH)
        return 0

    def greet_line(i, _):
        pl.semaphore_signal(barrier, inc=1, device_id=line_peer(i), device_id_type=MESH)
        return 0

    lax.fori_loop(0, ZLINE - 1, greet_line, 0)

    @pl.when(ghost)
    def _():
        for peer in (across_peer, greeter):
            pl.semaphore_signal(barrier, inc=1, device_id=peer, device_id_type=MESH)

    @pl.when(behind)
    def _():
        pl.semaphore_signal(barrier, inc=1, device_id=behind_peer, device_id_type=MESH)

    lax.fori_loop(0, PLANE - 1, greet_plane, 0)

    sends = (
        ((gx < SX - 1) & (gx != CY - 1), (gx + 1, gy, gz)),
        ((gx > 0) & (gx != CY), (gx - 1, gy, gz)),
        (gy < SY - 1, (gx, gy + 1, gz)),
        (gy > 0, (gx, gy - 1, gz)),
        (gz < SZ - 1, (gx, gy, gz + 1)),
        (gz > 0, (gx, gy, gz - 1)),
    )
    comes = (
        (gx > 0) & (gx != CY),
        (gx < SX - 1) & (gx != CY - 1),
        gy > 0,
        gy < SY - 1,
        gz > 0,
        gz < SZ - 1,
    )
    lands = (LOWX, jnp.where(gx == CY + 1, LOWX, UPX), LOWY, UPY, LOWZ, UPZ)
    deep_rows = {0: (48, 32), 1: (32, 16), 2: (32, 16), 3: (16, 16)}

    def rows_of(k, d, deep):
        return deep_rows[k][(d - 2) // 2] if deep else 16

    def halo(k, d, deep=False):
        x = x_one.at[k] if k < 2 else x_two.at[k - 2]
        faces = faces_one.at[k] if k < 2 else faces_two.at[k - 2]
        if d < 2:
            at = jnp.where(gx == CY, 0, LAYER) if d == 0 else 0
            src = x.at[pl.ds(pl.multiple_of(at, LAYER), LAYER)]
            dst = x.at[pl.ds(pl.multiple_of(lands[d], LAYER), LAYER)]
        else:
            size = rows_of(k, d, deep)
            src = faces.at[pl.ds(FACES[d - 2], size)]
            dst = x.at[pl.ds(lands[d], size)]
        return pltpu.make_async_remote_copy(
            src_ref=src,
            dst_ref=dst,
            send_sem=hs.at[k, d],
            recv_sem=hr.at[k, d],
            device_id=sends[d][1],
            device_id_type=MESH,
        )

    def for_halos(k, ways, conditions, act):
        for d in ways:
            if d < 2:
                @pl.when(conditions[d])
                def _():
                    act(halo(k, d))
            else:
                @pl.when(conditions[d] & ghost)
                def _():
                    act(halo(k, d, True))

                @pl.when(conditions[d] & jnp.logical_not(ghost))
                def _():
                    act(halo(k, d, False))

    def start_halos(k, ways=range(6)):
        for_halos(k, ways, [c for c, _ in sends], lambda copy: copy.start())

    def wait_halos(k, ways=range(6)):
        for_halos(k, ways, comes, lambda copy: copy.wait_recv())

    def far_copy(m):
        first = jnp.where(gx == CY + 1, 0, LAYER)
        at = (LAYER, 0, first, LAYER - first)[m]
        return pltpu.make_async_remote_copy(
            src_ref=x_one.at[0, pl.ds(pl.multiple_of(at, LAYER), LAYER)],
            dst_ref=x_one.at[0, pl.ds(UPX + m * LAYER, LAYER)],
            send_sem=fs.at[m],
            recv_sem=fr.at[m],
            device_id=across_peer if m < 2 else behind_peer,
            device_id_type=MESH,
        )

    def clear(at, size, first=True):
        for k in range(0 if first else 1, 2):
            x_one[k, pl.ds(at, size), :] = jnp.zeros((size, 2 * LANES), BF16)
        x_two[:, pl.ds(at, size), :] = jnp.zeros((2, size, 4 * LANES), BF16)

    clear(UPX + LAYER, 3 * LAYER, False)

    @pl.when(jnp.logical_not(ghost))
    def _():
        x_one[0, pl.ds(UPX + LAYER, 3 * LAYER), :] = jnp.zeros((3 * LAYER, 2 * LANES), BF16)
        for at, size in ((LOWY, 48), (UPY, 48), (LOWZ, 32), (UPZ, 32)):
            clear(at + 16, size - 16)

    @pl.when(ghost)
    def _():
        for k in range(1, ITERS):
            for d in range(2, 6):
                size, full = deep_rows[k][(d - 2) // 2], deep_rows[0][(d - 2) // 2]
                if size < full:
                    rest = pl.ds(lands[d] + size, full - size)
                    if k < 2:
                        x_one[k, rest, :] = jnp.zeros((full - size, 2 * LANES), BF16)
                    else:
                        x_two[k - 2, rest, :] = jnp.zeros((full - size, 4 * LANES), BF16)

    for absent, at, size in (
        (gx == 0, LOWX, LAYER),
        (gx == SX - 1, UPX, LAYER),
        (gy == 0, LOWY, 48),
        (gy == SY - 1, UPY, 48),
        (gz == 0, LOWZ, 32),
        (gz == SZ - 1, UPZ, 32),
    ):
        @pl.when(absent)
        def _():
            clear(at, size)

    own = (mirror, 1 - mirror)

    eye8 = iota((8, 8), 0) == iota((8, 8), 1)

    def column(row_of):
        return jnp.concatenate(
            [
                jnp.sum(
                    jnp.where(eye8, jnp.broadcast_to(row_of(own[a], b).astype(F32), (8, 8)), 0.0),
                    axis=1,
                    keepdims=True,
                )
                for a in range(NX)
                for b in range(NY)
            ],
            axis=0,
        )

    kinds = [column(lambda a, b: links[a, k, b : b + 1, :]) for k in range(7)]
    density = column(lambda a, b: dens[a, b : b + 1, :])
    owners = column(lambda a, b: owner[a, b : b + 1, :])

    eye = iota((DOF, DOF), 0) == iota((DOF, DOF), 1)
    eye_low = jnp.where(eye, 1.0, 0.0).astype(BF16)
    diagonals = []
    table[...] = jnp.zeros(table.shape, BF16)
    for t in range(4):
        block = selfb[t]
        diagonals.append(
            jnp.sum(jnp.where(eye, block.astype(F32), 0.0), axis=0, keepdims=True)
        )
        upper = lax.dot_general(eye_low, offb[t], NT_DIMS, preferred_element_type=F32)
        table[pl.ds(t * LANES, DOF), pl.ds(0, DOF)] = upper.astype(BF16)
        table[pl.ds((4 + t) * LANES, DOF), pl.ds(0, DOF)] = offb[t]
        table[pl.ds((8 + t) * LANES, DOF), pl.ds(0, DOF)] = block

    def prepare(at, size, kinds, density):
        scale = density * jnp.sqrt(density)
        pivots = jnp.ones((size, DOF), F32)
        for t in range(4):
            pivots = jnp.where(kinds[6] == float(t), diagonals[t], pivots)
        rows = pl.ds(at, size)
        rp[rows, :] = jnp.ones((size, LANES), F32)
        rp[rows, pl.ds(0, DOF)] = 1.0 / pivots
        sc[rows, :] = jnp.broadcast_to(scale, (size, LANES))
        su[rows, :] = rp[rows, :] * sc[rows, :]
        g = iota((size, 1), 0) + at
        gl, here, gyy, gzz = g // LAYER, g % LAYER, g // NZ % NY, g % NZ
        on, back = here + 2 * LAYER, here
        y, z = OUT + gl * NZ + gzz, OUT + gl * NY + gyy
        sources = (
            jnp.where(mirror == 1, back, on),
            jnp.where(gyy < NY - 1, here + LAYER + 8, y + FACES[1]),
            jnp.where(gzz < NZ - 1, here + LAYER + 1, z + FACES[3]),
            jnp.where(mirror == 1, on, back),
            jnp.where(gyy > 0, here + LAYER - 8, y + FACES[0]),
            jnp.where(gzz > 0, here + LAYER - 1, z + FACES[2]),
        )
        across = iota((size, SOURCES), 1).astype(F32)
        sources = [a.astype(F32) for a in sources]
        for side in range(2):
            for t in range(4):
                chosen = jnp.zeros((size, SOURCES), F32)
                for k in range(3 * side, 3 * side + 3):
                    code = jnp.where(kinds[k] == float(t), sources[k], -1.0)
                    chosen = jnp.where(across == code, 1.0, chosen)
                chosen = chosen.astype(BF16)
                for i in range(size // LAYER):
                    pick[at // LAYER + i, pl.ds((4 * side + t) * LAYER, LAYER), :] = chosen[
                        i * LAYER : (i + 1) * LAYER
                    ]

    prepare(0, G, kinds, density)

    v[0] = jnp.zeros((2 * G, LANES), F32)
    for a in range(NX):
        for f, load in enumerate((body, probe)):
            v[0, pl.ds(f * G + a * LAYER, LAYER), pl.ds(0, DOF)] = load[own[a]].reshape(LAYER, DOF)

    r = iota((FACE_ROWS, 1), 0)
    along_y, along_z = r % 48, r % 32
    face_y = along_y // 8 * LAYER + along_y % 8
    face_z = along_z // 4 * LAYER + along_z % 4 * 8
    face = jnp.where(
        r < 48, face_y + 24, jnp.where(r < 96, face_y, jnp.where(r < 128, face_z + 7, face_z))
    )
    outer = jnp.where(iota((FACE_ROWS, ALL), 1) == face, 1.0, 0.0).astype(BF16)

    def both(a):
        return jnp.concatenate([a, a], axis=0)

    def scaled(field, factor, parts):
        size = factor.shape[0]
        u = field * both(factor)
        high = u.astype(BF16)
        out = [high[:size], high[size:]]
        if parts == 2:
            low = (u - high.astype(F32)).astype(BF16)
            out += [low[:size], low[size:]]
        return out

    def fold(a, size):
        return a[: 2 * size] + a[2 * size :] if a.shape[0] == 4 * size else a

    def straight(parts, kind):
        size = kind.shape[0]
        masks = [jnp.broadcast_to(kind == float(t), (size, LANES)) for t in range(4)]
        left = []
        for part in parts:
            part = part.astype(F32)
            left.append(
                jnp.concatenate([jnp.where(m, part, 0.0).astype(BF16) for m in masks], axis=1)
            )
        left = jnp.concatenate(left, axis=0)
        return fold(
            jnp.dot(left, table[pl.ds(8 * LANES, 4 * LANES)], preferred_element_type=F32), size
        )

    def coupled(sources):
        size = len(sources) * LAYER
        highs, lows = ([], []), ([], [])
        for i, source in enumerate(sources):
            z = jnp.dot(pick[i], source, preferred_element_type=F32)
            if z.shape[1] == 4 * LANES:
                z = z[:, : 2 * LANES] + z[:, 2 * LANES :]
            high = z.astype(BF16)
            low = (z - high.astype(F32)).astype(BF16)
            for f in range(2):
                for a, out in ((high, highs), (low, lows)):
                    out[f].append(
                        jnp.concatenate(
                            [
                                a[t * LAYER : (t + 1) * LAYER, f * LANES : (f + 1) * LANES]
                                for t in range(8)
                            ],
                            axis=1,
                        )
                    )
        left = jnp.concatenate(highs[0] + highs[1] + lows[0] + lows[1], axis=0)
        return fold(jnp.dot(left, table[pl.ds(0, 8 * LANES)], preferred_element_type=F32), size)

    def sources_of(k, layers):
        def rows(at, size):
            return x_one[k, pl.ds(at, size), :] if k < 2 else x_two[k - 2, pl.ds(at, size), :]

        outside = rows(LOWY, FACE_ROWS)
        out = []
        for i in range(layers):
            near = (
                [rows(LOWX, LAYER), rows(0, 2 * LAYER)]
                if i == 0
                else [rows((i - 1) * LAYER, 3 * LAYER)]
            )
            out.append(jnp.concatenate(near + [outside], axis=0))
        return out

    def faces_of(sent):
        return jnp.dot(
            outer[:, : sent.shape[0]], sent, preferred_element_type=F32
        ).astype(BF16)

    def ship(k):
        more = (ITERS - k) * LAYER
        own_parts = scaled(v[k], su[pl.ds(0, G), :], 1 if k < 2 else 2)
        far_parts = scaled(
            jnp.concatenate([vg[f, pl.ds(0, more), :] for f in range(2)], axis=0),
            su[pl.ds(G, more), :],
            1 if k < 2 else 2,
        )
        sent = jnp.concatenate(own_parts, axis=1)
        beyond = jnp.concatenate(far_parts, axis=1)
        x, i = (x_one, k) if k < 2 else (x_two, k - 2)
        x[i, pl.ds(0, G), :] = sent

        @pl.when(ghost)
        def _():
            x[i, pl.ds(UPX, more), :] = beyond

        (faces_one if k < 2 else faces_two)[i] = faces_of(
            jnp.concatenate([sent, beyond], axis=0)
        )
        last = more - LAYER
        return [
            jnp.concatenate([a, b[:last]], axis=0) if last else a
            for a, b in zip(own_parts, far_parts)
        ]

    def gram(fields, i, j):
        product = fields[i] * fields[j]
        for f in range(2):
            part = jnp.sum(product[f * G : (f + 1) * G], axis=0, keepdims=True)
            rr[pl.ds(f * 16 + place(i, j), 1), :] = part[:, :128] + part[:, 128:]

    def gram_rows():
        sums = jnp.sum(rr[...], axis=1, keepdims=True)
        spot = iota((16, 128), 0) == iota((16, 128), 1)
        return [
            jnp.sum(jnp.where(spot, sums[f * 16 : f * 16 + 16], 0.0), axis=0, keepdims=True)
            for f in range(2)
        ]

    def start_plane(e):
        def one(i, _):
            if e == 0:
                src, dst = mp, mps.at[PLANE - 2 - i]
            elif e == 1:
                src, dst = mq, mqs.at[PLANE - 2 - i]
            else:
                src, dst = me, mes.at[PLANE - 2 - i]
            pltpu.make_async_remote_copy(
                src_ref=src, dst_ref=dst, send_sem=ps.at[e], recv_sem=pr.at[e],
                device_id=plane_peer(i), device_id_type=MESH,
            ).start()
            return 0

        lax.fori_loop(0, PLANE - 1, one, 0)

    def start_line(e):
        for o in sorted(range(1, ZLINE), key=lambda o: -min(o, ZLINE - o)):
            i = o - 1
            if e == 0:
                src, dst = mz, mzs.at[ZLINE - 2 - i]
            else:
                src, dst = tile.at[(me_z + o) % ZLINE], tiles.at[ZLINE - 2 - i]
            pltpu.make_async_remote_copy(
                src_ref=src, dst_ref=dst, send_sem=zs.at[e], recv_sem=zr.at[e],
                device_id=line_peer(i), device_id_type=MESH,
            ).start()

    def wait_all(buffer, sem):
        pltpu.make_async_copy(buffer, buffer, sem).wait()

    rr[...] = jnp.zeros(rr.shape, F32)
    sent = scaled(v[0], su[pl.ds(0, G), :], 1)

    def split3(a):
        first = a.astype(BF16).astype(F32)
        second = (a - first).astype(BF16).astype(F32)
        return [first, second, a - first - second]

    lane = iota((G, LANES), 1)
    notes = sent[0].astype(F32)
    for i, col in enumerate(kinds + split3(density)):
        notes = jnp.where(lane == DOF + i, col, notes)
    sent = jnp.concatenate([notes.astype(BF16), sent[1]], axis=1)
    x_one[0, pl.ds(0, G), :] = sent

    @pl.when(jnp.logical_not(ghost))
    def _():
        faces_one[0] = faces_of(sent)


    inner = [v[0]]
    for _ in range(ITERS - 1):
        parts = scaled(inner[-1], su[pl.ds(0, G), :], 1)
        near = jnp.concatenate(parts, axis=1)

        def empty(size):
            return jnp.zeros((size, 2 * LANES), BF16)

        moved = LOCAL_GAIN * coupled(
            [
                jnp.concatenate([empty(LAYER), near, empty(FACE_ROWS)], axis=0),
                jnp.concatenate([near, empty(LAYER + FACE_ROWS)], axis=0),
            ]
        )
        inner.append((moved + straight(parts, kinds[6])) * both(sc[pl.ds(0, G), :]))
    for i in range(ITERS):
        for j in range(i, ITERS):
            gram(inner, i, j)

    spread = iota((G, 128), 1) == iota((G, 128), 0)

    def as_row(col):
        return jnp.sum(jnp.where(spread, col, 0.0), axis=0, keepdims=True)

    rows = gram_rows()
    mp[0:1, :] = rows[0]
    mp[1:2, :] = rows[1]
    mp[2:3, :] = as_row(owners)
    mp[3:4, :] = as_row(density)

    extra = 2 * ghost.astype(jnp.int32) + behind.astype(jnp.int32)
    pl.semaphore_wait(barrier, PLANE - 1 + ZLINE - 1 + extra)

    @pl.when(ghost)
    def _():
        for m in range(2):
            far_copy(m).start()

    @pl.when(behind)
    def _():
        for m in range(2, 4):
            far_copy(m).start()

    start_halos(0, (0, 1))

    @pl.when(jnp.logical_not(ghost))
    def _():
        for d in range(2, 6):
            @pl.when(sends[d][0])
            def _():
                halo(0, d).start()

    start_plane(0)
    wait_all(mps, pr.at[0])
    mz[...] = mp[...] + total(mps[i] for i in range(PLANE - 1))
    start_line(0)

    low_half = iota((1, 128), 1) < G

    def joined(a, b):
        return jnp.where(low_half, a, pltpu.roll(b, G, 1))

    def gathered(row):
        parts = [mps[i, row : row + 1, :] for i in range(PLANE - 1)]
        parts.append(mp[row : row + 1, :])
        return [joined(parts[2 * m], parts[2 * m + 1]) for m in range(PLANE // 2)]

    q = iota((128, 1), 0)
    bins = (((q // 64 * CY + yc) * SY + gy) * SZ + q // 8 % 8) * GPB + q % 8
    bins = bins.astype(F32)
    for m, row in enumerate(gathered(2)):
        hot[:, pl.ds(m * 128, 128)] = jnp.where(row == bins, 1.0, 0.0).astype(BF16)

    masses = gathered(3)
    split[pl.ds(96, 32), :] = jnp.zeros((32, PLANE * G), BF16)

    wait_halos(0, (0, 1))

    @pl.when(ghost)
    def _():
        for m in range(4):
            far_copy(m).wait_recv()
        faces_one[0] = faces_of(x_one[0, pl.ds(0, ALL), :])
        for d in range(2, 6):
            @pl.when(sends[d][0])
            def _():
                halo(0, d, True).start()

    notes = x_one[0, pl.ds(UPX, DEEP * LAYER), pl.ds(128, 128)].astype(F32)
    notes = [notes[:, DOF - 128 + i : DOF - 127 + i] for i in range(10)]
    prepare(G, DEEP * LAYER, notes[:7], notes[7] + notes[8] + notes[9])
    kind = jnp.concatenate([kinds[6], notes[6]], axis=0)
    beyond = su[pl.ds(G, DEEP * LAYER), :]
    beyond = jnp.where(beyond > 0.0, 1.0 / beyond, 0.0)
    parts = []
    for f in range(2):
        parts.append(x_one[0, pl.ds(0, ALL), pl.ds(f * LANES, LANES)])
        vg[f] = parts[f][G:].astype(F32) * beyond

    spots = {}
    for i in range(ITERS):
        for j in range(ITERS):
            n = len(spots)
            spots[i, j] = n % 8 + 16 * (n // 8)
    for i in range(ITERS):
        spots[i, ITERS] = 8 + i
        spots[ITERS, i] = 24 + i
    lane = iota((G, 128), 1)
    columns = [jnp.zeros((G, 128), F32)]

    def products(i, j):
        part = v[i, pl.ds(G, G), :] * rp[pl.ds(0, G), :] * v[j, pl.ds(0, G), :]
        col = jnp.sum(part, axis=1, keepdims=True)
        columns[0] = jnp.where(lane == spots[i, j], col, columns[0])

    def turned(at):
        rows = jnp.transpose(jnp.concatenate([columns[0], jnp.zeros((G, 128), F32)], axis=0))
        return jnp.where(
            low_half, rows[at : at + 8], pltpu.roll(rows[at + 16 : at + 24], G, 1)
        )

    guess = None
    for k in range(ITERS):
        size = ALL - k * LAYER
        alone = straight(parts, kind[:size])
        wait_halos(k, range(2, 6) if k == 0 else range(6))
        moved = (coupled(sources_of(k, size // LAYER)) + alone) * both(sc[pl.ds(0, size), :])
        ours = jnp.concatenate([moved[:G], moved[size : size + G]], axis=0)
        if k == 0:
            wait_all(mzs, zr.at[0])
            row = mz[0:2, :] + total(mzs[i, 0:2, :] for i in range(ZLINE - 1))
            guess, _, _ = sweeps(
                entries(row, ITERS), ITERS - 1, lambda c: {i + 1: e for i, e in c.items()}
            )
            guess = [jnp.where((s > 1e-3) & (s < 1e6), s, 1.0) for s in guess]
        if k < ITERS - 1:
            step = jnp.concatenate(
                [jnp.broadcast_to(guess[k][f : f + 1], (G, 1)) for f in range(2)], axis=0
            )
            v[k + 1] = v[k] - step * ours
            for f in range(2):
                more = size - G
                vg[f, pl.ds(0, more), :] = (
                    vg[f, pl.ds(0, more), :]
                    - guess[k][f : f + 1] * moved[f * size + G : (f + 1) * size]
                )
            parts = ship(k + 1)
            start_halos(k + 1)
        else:
            v[k + 1] = ours
        for i in range(k + 2):
            gram(v, i, k + 1)
        if k == 0:
            gram(v, 0, 0)
            products(0, 0)
        for i in range(k + 1):
            products(i, k + 1)
            products(k + 1, i)
        if 0 < k + 1 < ITERS:
            products(k + 1, k + 1)
        if k == ITERS - 2:
            me[...] = turned(0)
            start_plane(2)

    rows = gram_rows()
    mq[...] = turned(8)
    mq[4:5, :] = rows[0]
    mq[5:6, :] = rows[1]
    start_plane(1)
    wait_all(mes, pr.at[2])
    wait_all(mqs, pr.at[1])
    sums = mq[4:6, :] + total(mqs[i, 4:6, :] for i in range(PLANE - 1))

    def message(i):
        parts = [mes[i], mqs[i]] if i < PLANE - 1 else [me[...], mq[...]]
        return jnp.concatenate(parts, axis=0)

    sub = iota((16, 128), 0)
    for m in range(PLANE // 2):
        a, b = message(2 * m), message(2 * m + 1)
        low = jnp.where(low_half, a, pltpu.roll(b, G, 1))
        high = jnp.where(low_half, pltpu.roll(a, G, 1), b)
        low = jnp.where(sub < 12, low, jnp.where(sub == 12, masses[m], 0.0))
        high = jnp.where(sub < 12, high, 0.0)
        for i, part in enumerate(split3(jnp.concatenate([low, high], axis=0))):
            split[pl.ds(i * 32, 32), pl.ds(m * 128, 128)] = part.astype(BF16)
    blocks = lax.dot_general(hot[...], split[...], NT_DIMS, preferred_element_type=F32)
    blocks = blocks + pltpu.roll(blocks, 96, 1) + pltpu.roll(blocks, 64, 1)
    lane = iota((8, 128), 1)
    first = iota((8, 128), 0) == 0
    shared = jnp.where(
        first & (lane >= 32) & (lane < 48),
        pltpu.roll(sums, 32, 1)[0:1],
        jnp.where(first & (lane >= 48) & (lane < 64), pltpu.roll(sums, 48, 1)[1:2], 0.0),
    )
    for i in range(ZLINE):
        full = jnp.where(lane < 32, blocks[i * 8 : (i + 1) * 8], shared)
        tile[i] = jnp.where(low_half, full[0:4], pltpu.roll(full, G, 1)[4:8])
    start_line(1)
    wait_all(tiles, zr.at[1])
    mine = tile[me_z] + total(tiles[i] for i in range(ZLINE - 1))
    mine = jnp.concatenate([mine, pltpu.roll(mine, G, 1)], axis=0)
    row = jnp.concatenate(
        [pltpu.roll(mine, 96, 1)[0:1], pltpu.roll(mine, 80, 1)[0:1]], axis=0
    )

    inverse = [1.0 / s for s in guess]

    def newton(c):
        out = {}
        for i, e in c.items():
            if i < ITERS - 1:
                part = e * inverse[i]
                out[i] = out[i] + part if i in out else part
                out[i + 1] = out[i + 1] - part if i + 1 in out else -part
            else:
                out[i + 1] = e
        return out

    _, answer, left = sweeps(entries(row, ITERS + 1), ITERS, newton)

    def combine(coefficients, f):
        return total(
            c[f : f + 1, :] * v[i, pl.ds(f * G, G), :] for i, c in coefficients.items()
        )

    solved = [combine(answer, f) * rp[pl.ds(0, G), :] for f in range(2)]
    for a in range(NX):
        for f, out in enumerate((state_out, adjoint_out)):
            out[own[a]] = solved[f][a * LAYER : (a + 1) * LAYER, :DOF].reshape(NY, NZ, DOF)
    applied = {i: (1.0 - c if i == 0 else -c) for i, c in left.items()}
    lane = iota((1, 128), 1)
    weights = jnp.zeros((1, 128), F32)
    for (i, j), spot in spots.items():
        terms = []
        if i < ITERS:
            terms.append(answer[i][1:2] * applied[j][0:1])
        if j < ITERS:
            terms.append(answer[j][0:1] * applied[i][1:2])
        weights = jnp.where(lane == spot, total(terms), weights)
    above = -1.5 * jnp.sum(mine * weights, axis=1, keepdims=True)
    below = mine[:, 12:13]
    ratio = jnp.where(below > 0.0, above / below, 0.0)
    coarse_out[...] = jnp.sum(jnp.where(eye8, ratio, 0.0), axis=0, keepdims=True)

    for k in range(ITERS):
        for_halos(k, range(6), [c for c, _ in sends], lambda copy: copy.wait_send())

    @pl.when(ghost)
    def _():
        for m in range(2):
            far_copy(m).wait_send()

    @pl.when(behind)
    def _():
        for m in range(2, 4):
            far_copy(m).wait_send()

    for buffer, sem in (
        (mps, ps.at[0]),
        (mqs, ps.at[1]),
        (mes, ps.at[2]),
        (mzs, zs.at[0]),
        (tiles, zs.at[1]),
    ):
        wait_all(buffer, sem)


def deliver(state, adjoint, coarse, state_out, adjoint_out, coarse_out):
    state_out[...] = state[...]
    adjoint_out[...] = adjoint[...]
    coarse_out[...] = coarse[...]


def local(body_load, probe_load, density, link_types, off_blocks, self_blocks, block_owner):
    vmem = pl.BlockSpec(memory_space=pltpu.VMEM)
    state, adjoint, coarse = pl.pallas_call(
        kernel,
        out_shape=(
            jax.ShapeDtypeStruct(body_load.shape, F32),
            jax.ShapeDtypeStruct(body_load.shape, F32),
            jax.ShapeDtypeStruct((1, GPB), F32),
        ),
        in_specs=[vmem] * 7,
        out_specs=(vmem,) * 3,
        scratch_shapes=[
            pltpu.VMEM((2, ROWS, 2 * LANES), BF16),
            pltpu.VMEM((2, ROWS, 4 * LANES), BF16),
            pltpu.VMEM((2, FACE_ROWS, 2 * LANES), BF16),
            pltpu.VMEM((2, FACE_ROWS, 4 * LANES), BF16),
            pltpu.VMEM((2, DEEP * LAYER, LANES), F32),
            pltpu.VMEM((5, 8 * LAYER, SOURCES), BF16),
            pltpu.VMEM((12 * LANES, LANES), BF16),
            pltpu.VMEM((ITERS + 1, 2 * G, LANES), F32),
            pltpu.VMEM((ALL, LANES), F32),
            pltpu.VMEM((ALL, LANES), F32),
            pltpu.VMEM((ALL, LANES), F32),
            pltpu.VMEM((128, PLANE * G), BF16),
            pltpu.VMEM((32, 128), F32),
            pltpu.VMEM((4, 128), F32),
            pltpu.VMEM((PLANE - 1, 4, 128), F32),
            pltpu.VMEM((4, 128), F32),
            pltpu.VMEM((ZLINE - 1, 4, 128), F32),
            pltpu.VMEM((8, 128), F32),
            pltpu.VMEM((PLANE - 1, 8, 128), F32),
            pltpu.VMEM((8, 128), F32),
            pltpu.VMEM((PLANE - 1, 8, 128), F32),
            pltpu.VMEM((128, PLANE * G), BF16),
            pltpu.VMEM((ZLINE, 4, 128), F32),
            pltpu.VMEM((ZLINE - 1, 4, 128), F32),
            pltpu.SemaphoreType.DMA((ITERS, 6)),
            pltpu.SemaphoreType.DMA((ITERS, 6)),
            pltpu.SemaphoreType.DMA((4,)),
            pltpu.SemaphoreType.DMA((4,)),
            pltpu.SemaphoreType.DMA((3,)),
            pltpu.SemaphoreType.DMA((3,)),
            pltpu.SemaphoreType.DMA((2,)),
            pltpu.SemaphoreType.DMA((2,)),
        ],
        compiler_params=pltpu.CompilerParams(
            collective_id=0, has_side_effects=True, vmem_limit_bytes=60 << 20
        ),
        name="sweeps",
    )(
        body_load,
        probe_load,
        density,
        jnp.transpose(link_types, (0, 3, 1, 2)),
        off_blocks,
        self_blocks,
        block_owner,
    )
    state, adjoint, coarse = pl.pallas_call(
        deliver,
        out_shape=(
            jax.ShapeDtypeStruct(body_load.shape, F32),
            jax.ShapeDtypeStruct(body_load.shape, F32),
            jax.ShapeDtypeStruct((1, GPB), F32),
        ),
        in_specs=[vmem] * 3,
        out_specs=(vmem,) * 3,
        name="deliver",
    )(state, adjoint, coarse)
    return state, adjoint, coarse.reshape(GPB)


def solution(mesh):
    in_specs = (
        P("gx", "gy", "gz", None),
        P("gx", "gy", "gz", None),
        P("gx", "gy", "gz"),
        P("gx", "gy", "gz", None),
        P(),
        P(),
        P("gx", "gy", "gz"),
    )
    out_specs = (P("gx", "gy", "gz", None), P("gx", "gy", "gz", None), P(("gx", "gy", "gz")))
    return jax.shard_map(local, mesh=mesh, in_specs=in_specs, out_specs=out_specs, check_vma=False)
```

```python
import functools

import jax
import jax.numpy as jnp
from jax import lax
from jax.experimental import pallas as pl
from jax.experimental.pallas import tpu as pltpu
from jax.sharding import PartitionSpec as P

MESH = pl.DeviceIdType.MESH
F32, BF16 = jnp.float32, jnp.bfloat16
ITERS = 4
GPB = 8
NX, NY, NZ = 2, 4, 8
G = NX * NY * NZ
DOF, LANES = 192, 256
LAYER, DEEP = NY * NZ, 3
ALL = G + DEEP * LAYER
UPX, LOWX, LOWY, UPY, LOWZ, UPZ, ROWS = 64, 192, 224, 272, 320, 352, 384
FACES = (0, 48, 96, 128)
FACE_ROWS = 160
OUT, SOURCES = 96, 256
SX, SY, SZ, CY = 16, 4, 8, 8
PLANE, ZLINE = 32, 16
LOCAL_GAIN = (3 / 2.125) ** 0.5
NT_DIMS = (((1,), (1,)), ((), ()))


def iota(shape, dim):
    return lax.broadcasted_iota(jnp.int32, shape, dim)


def total(values):
    values = list(values)
    while len(values) > 1:
        pairs = [values[i] + values[i + 1] for i in range(0, len(values) - 1, 2)]
        values = pairs + values[len(pairs) * 2 :]
    return values[0]


def place(i, j):
    i, j = min(i, j), max(i, j)
    return i * 5 - i * (i - 1) // 2 + (j - i)


def entries(row, size):
    lane = iota(row.shape, 1)
    table = {}
    for i in range(size):
        for j in range(i, size):
            table[i, j] = table[j, i] = jnp.sum(
                jnp.where(lane == place(i, j), row, 0.0), axis=1, keepdims=True
            )
    return table


def bilinear(left, table, right):
    return total(
        left[i] * total(table[i, j] * right[j] for j in right) for i in left
    )


def sweeps(table, count, image):
    one = jnp.ones_like(table[0, 0])
    residual, answer, steps = {0: one}, {}, []
    for _ in range(count):
        moved = image(residual)
        projected = bilinear(residual, table, moved)
        energy = bilinear(moved, table, moved)
        step = projected / (energy + 1e-6)
        steps.append(step)
        for i, c in residual.items():
            answer[i] = answer[i] + step * c if i in answer else step * c
        for i, c in moved.items():
            residual[i] = residual[i] - step * c if i in residual else -(step * c)
    return steps, answer, residual


def kernel(body, probe, dens, links, offb, selfb, owner, state_out, adjoint_out, coarse_out,
           x_one, x_two, faces_one, faces_two, vg, pick, table, v, su, sc, rp, hot, rr, mp, mps, mz, mzs, mq, mqs, me, mes, split, tile, tiles,
           hs, hr, fs, fr, ps, pr, zs, zr):
    gx, gy, gz = lax.axis_index("gx"), lax.axis_index("gy"), lax.axis_index("gz")
    zh, yc = gx // CY, gx % CY
    me_p = yc * SY + gy
    me_z = zh * SZ + gz
    ghost = jnp.logical_or(gx == CY - 1, gx == CY)
    behind = jnp.logical_or(gx == CY - 2, gx == CY + 1)
    mirror = (gx == CY).astype(jnp.int32)
    across_peer = (2 * CY - 1 - gx, gy, gz)
    behind_peer = (jnp.where(gx == CY + 1, CY - 1, CY), gy, gz)
    greeter = (jnp.where(gx == CY, CY - 2, CY + 1), gy, gz)

    def plane_peer(i):
        p = (me_p + 1 + i) % PLANE
        return (zh * CY + p // SY, p % SY, gz)

    def line_peer(i):
        q = (me_z + 1 + i) % ZLINE
        return (q // SZ * CY + yc, gy, q % SZ)

    barrier = pltpu.get_barrier_semaphore()

    def greet_plane(i, _):
        pl.semaphore_signal(barrier, inc=1, device_id=plane_peer(i), device_id_type=MESH)
        return 0

    def greet_line(i, _):
        pl.semaphore_signal(barrier, inc=1, device_id=line_peer(i), device_id_type=MESH)
        return 0

    lax.fori_loop(0, ZLINE - 1, greet_line, 0)

    @pl.when(ghost)
    def _():
        for peer in (across_peer, greeter):
            pl.semaphore_signal(barrier, inc=1, device_id=peer, device_id_type=MESH)

    @pl.when(behind)
    def _():
        pl.semaphore_signal(barrier, inc=1, device_id=behind_peer, device_id_type=MESH)

    lax.fori_loop(0, PLANE - 1, greet_plane, 0)

    sends = (
        ((gx < SX - 1) & (gx != CY - 1), (gx + 1, gy, gz)),
        ((gx > 0) & (gx != CY), (gx - 1, gy, gz)),
        (gy < SY - 1, (gx, gy + 1, gz)),
        (gy > 0, (gx, gy - 1, gz)),
        (gz < SZ - 1, (gx, gy, gz + 1)),
        (gz > 0, (gx, gy, gz - 1)),
    )
    comes = (
        (gx > 0) & (gx != CY),
        (gx < SX - 1) & (gx != CY - 1),
        gy > 0,
        gy < SY - 1,
        gz > 0,
        gz < SZ - 1,
    )
    lands = (LOWX, jnp.where(gx == CY + 1, LOWX, UPX), LOWY, UPY, LOWZ, UPZ)
    deep_rows = {0: (48, 32), 1: (32, 16), 2: (32, 16), 3: (16, 16)}

    def rows_of(k, d, deep):
        return deep_rows[k][(d - 2) // 2] if deep else 16

    def halo(k, d, deep=False):
        x = x_one.at[k] if k < 2 else x_two.at[k - 2]
        faces = faces_one.at[k] if k < 2 else faces_two.at[k - 2]
        if d < 2:
            at = jnp.where(gx == CY, 0, LAYER) if d == 0 else 0
            src = x.at[pl.ds(pl.multiple_of(at, LAYER), LAYER)]
            dst = x.at[pl.ds(pl.multiple_of(lands[d], LAYER), LAYER)]
        else:
            size = rows_of(k, d, deep)
            src = faces.at[pl.ds(FACES[d - 2], size)]
            dst = x.at[pl.ds(lands[d], size)]
        return pltpu.make_async_remote_copy(
            src_ref=src,
            dst_ref=dst,
            send_sem=hs.at[k, d],
            recv_sem=hr.at[k, d],
            device_id=sends[d][1],
            device_id_type=MESH,
        )

    def for_halos(k, ways, conditions, act):
        for d in ways:
            if d < 2:
                @pl.when(conditions[d])
                def _():
                    act(halo(k, d))
            else:
                @pl.when(conditions[d] & ghost)
                def _():
                    act(halo(k, d, True))

                @pl.when(conditions[d] & jnp.logical_not(ghost))
                def _():
                    act(halo(k, d, False))

    def start_halos(k, ways=range(6)):
        for_halos(k, ways, [c for c, _ in sends], lambda copy: copy.start())

    def wait_halos(k, ways=range(6)):
        for_halos(k, ways, comes, lambda copy: copy.wait_recv())

    def far_copy(m):
        first = jnp.where(gx == CY + 1, 0, LAYER)
        at = (LAYER, 0, first, LAYER - first)[m]
        return pltpu.make_async_remote_copy(
            src_ref=x_one.at[0, pl.ds(pl.multiple_of(at, LAYER), LAYER)],
            dst_ref=x_one.at[0, pl.ds(UPX + m * LAYER, LAYER)],
            send_sem=fs.at[m],
            recv_sem=fr.at[m],
            device_id=across_peer if m < 2 else behind_peer,
            device_id_type=MESH,
        )

    def clear(at, size, first=True):
        for k in range(0 if first else 1, 2):
            x_one[k, pl.ds(at, size), :] = jnp.zeros((size, 2 * LANES), BF16)
        x_two[:, pl.ds(at, size), :] = jnp.zeros((2, size, 4 * LANES), BF16)

    clear(UPX + LAYER, 3 * LAYER, False)

    @pl.when(jnp.logical_not(ghost))
    def _():
        x_one[0, pl.ds(UPX + LAYER, 3 * LAYER), :] = jnp.zeros((3 * LAYER, 2 * LANES), BF16)
        for at, size in ((LOWY, 48), (UPY, 48), (LOWZ, 32), (UPZ, 32)):
            clear(at + 16, size - 16)

    @pl.when(ghost)
    def _():
        for k in range(1, ITERS):
            for d in range(2, 6):
                size, full = deep_rows[k][(d - 2) // 2], deep_rows[0][(d - 2) // 2]
                if size < full:
                    rest = pl.ds(lands[d] + size, full - size)
                    if k < 2:
                        x_one[k, rest, :] = jnp.zeros((full - size, 2 * LANES), BF16)
                    else:
                        x_two[k - 2, rest, :] = jnp.zeros((full - size, 4 * LANES), BF16)

    for absent, at, size in (
        (gx == 0, LOWX, LAYER),
        (gx == SX - 1, UPX, LAYER),
        (gy == 0, LOWY, 48),
        (gy == SY - 1, UPY, 48),
        (gz == 0, LOWZ, 32),
        (gz == SZ - 1, UPZ, 32),
    ):
        @pl.when(absent)
        def _():
            clear(at, size)

    own = (mirror, 1 - mirror)

    eye8 = iota((8, 8), 0) == iota((8, 8), 1)

    def column(row_of):
        return jnp.concatenate(
            [
                jnp.sum(
                    jnp.where(eye8, jnp.broadcast_to(row_of(own[a], b).astype(F32), (8, 8)), 0.0),
                    axis=1,
                    keepdims=True,
                )
                for a in range(NX)
                for b in range(NY)
            ],
            axis=0,
        )

    kinds = [column(lambda a, b: links[a, k, b : b + 1, :]) for k in range(7)]
    density = column(lambda a, b: dens[a, b : b + 1, :])
    owners = column(lambda a, b: owner[a, b : b + 1, :])

    eye = iota((DOF, DOF), 0) == iota((DOF, DOF), 1)
    eye_low = jnp.where(eye, 1.0, 0.0).astype(BF16)
    diagonals = []
    table[...] = jnp.zeros(table.shape, BF16)
    for t in range(4):
        block = selfb[t]
        diagonals.append(
            jnp.sum(jnp.where(eye, block.astype(F32), 0.0), axis=0, keepdims=True)
        )
        upper = lax.dot_general(eye_low, offb[t], NT_DIMS, preferred_element_type=F32)
        table[pl.ds(t * LANES, DOF), pl.ds(0, DOF)] = upper.astype(BF16)
        table[pl.ds((4 + t) * LANES, DOF), pl.ds(0, DOF)] = offb[t]
        table[pl.ds((8 + t) * LANES, DOF), pl.ds(0, DOF)] = block

    def prepare(at, size, kinds, density):
        scale = density * jnp.sqrt(density)
        pivots = jnp.ones((size, DOF), F32)
        for t in range(4):
            pivots = jnp.where(kinds[6] == float(t), diagonals[t], pivots)
        rows = pl.ds(at, size)
        rp[rows, :] = jnp.ones((size, LANES), F32)
        rp[rows, pl.ds(0, DOF)] = 1.0 / pivots
        sc[rows, :] = jnp.broadcast_to(scale, (size, LANES))
        su[rows, :] = rp[rows, :] * sc[rows, :]
        g = iota((size, 1), 0) + at
        gl, here, gyy, gzz = g // LAYER, g % LAYER, g // NZ % NY, g % NZ
        on, back = here + 2 * LAYER, here
        y, z = OUT + gl * NZ + gzz, OUT + gl * NY + gyy
        sources = (
            jnp.where(mirror == 1, back, on),
            jnp.where(gyy < NY - 1, here + LAYER + 8, y + FACES[1]),
            jnp.where(gzz < NZ - 1, here + LAYER + 1, z + FACES[3]),
            jnp.where(mirror == 1, on, back),
            jnp.where(gyy > 0, here + LAYER - 8, y + FACES[0]),
            jnp.where(gzz > 0, here + LAYER - 1, z + FACES[2]),
        )
        across = iota((size, SOURCES), 1).astype(F32)
        sources = [a.astype(F32) for a in sources]
        for side in range(2):
            for t in range(4):
                chosen = jnp.zeros((size, SOURCES), F32)
                for k in range(3 * side, 3 * side + 3):
                    code = jnp.where(kinds[k] == float(t), sources[k], -1.0)
                    chosen = jnp.where(across == code, 1.0, chosen)
                chosen = chosen.astype(BF16)
                for i in range(size // LAYER):
                    pick[at // LAYER + i, pl.ds((4 * side + t) * LAYER, LAYER), :] = chosen[
                        i * LAYER : (i + 1) * LAYER
                    ]

    prepare(0, G, kinds, density)

    v[0] = jnp.zeros((2 * G, LANES), F32)
    for a in range(NX):
        for f, load in enumerate((body, probe)):
            v[0, pl.ds(f * G + a * LAYER, LAYER), pl.ds(0, DOF)] = load[own[a]].reshape(LAYER, DOF)

    r = iota((FACE_ROWS, 1), 0)
    along_y, along_z = r % 48, r % 32
    face_y = along_y // 8 * LAYER + along_y % 8
    face_z = along_z // 4 * LAYER + along_z % 4 * 8
    face = jnp.where(
        r < 48, face_y + 24, jnp.where(r < 96, face_y, jnp.where(r < 128, face_z + 7, face_z))
    )
    outer = jnp.where(iota((FACE_ROWS, ALL), 1) == face, 1.0, 0.0).astype(BF16)

    def both(a):
        return jnp.concatenate([a, a], axis=0)

    def scaled(field, factor, parts):
        size = factor.shape[0]
        u = field * both(factor)
        high = u.astype(BF16)
        out = [high[:size], high[size:]]
        if parts == 2:
            low = (u - high.astype(F32)).astype(BF16)
            out += [low[:size], low[size:]]
        return out

    def fold(a, size):
        return a[: 2 * size] + a[2 * size :] if a.shape[0] == 4 * size else a

    def straight(parts, kind):
        size = kind.shape[0]
        masks = [jnp.broadcast_to(kind == float(t), (size, LANES)) for t in range(4)]
        left = []
        for part in parts:
            part = part.astype(F32)
            left.append(
                jnp.concatenate([jnp.where(m, part, 0.0).astype(BF16) for m in masks], axis=1)
            )
        left = jnp.concatenate(left, axis=0)
        return fold(
            jnp.dot(left, table[pl.ds(8 * LANES, 4 * LANES)], preferred_element_type=F32), size
        )

    def coupled(sources):
        size = len(sources) * LAYER
        highs, lows = ([], []), ([], [])
        for i, source in enumerate(sources):
            z = jnp.dot(pick[i], source, preferred_element_type=F32)
            if z.shape[1] == 4 * LANES:
                z = z[:, : 2 * LANES] + z[:, 2 * LANES :]
            high = z.astype(BF16)
            low = (z - high.astype(F32)).astype(BF16)
            for f in range(2):
                for a, out in ((high, highs), (low, lows)):
                    out[f].append(
                        jnp.concatenate(
                            [
                                a[t * LAYER : (t + 1) * LAYER, f * LANES : (f + 1) * LANES]
                                for t in range(8)
                            ],
                            axis=1,
                        )
                    )
        left = jnp.concatenate(highs[0] + highs[1] + lows[0] + lows[1], axis=0)
        return fold(jnp.dot(left, table[pl.ds(0, 8 * LANES)], preferred_element_type=F32), size)

    def sources_of(k, layers):
        def rows(at, size):
            return x_one[k, pl.ds(at, size), :] if k < 2 else x_two[k - 2, pl.ds(at, size), :]

        outside = rows(LOWY, FACE_ROWS)
        out = []
        for i in range(layers):
            near = (
                [rows(LOWX, LAYER), rows(0, 2 * LAYER)]
                if i == 0
                else [rows((i - 1) * LAYER, 3 * LAYER)]
            )
            out.append(jnp.concatenate(near + [outside], axis=0))
        return out

    def faces_of(sent):
        return jnp.dot(
            outer[:, : sent.shape[0]], sent, preferred_element_type=F32
        ).astype(BF16)

    def ship(k):
        more = (ITERS - k) * LAYER
        own_parts = scaled(v[k], su[pl.ds(0, G), :], 1 if k < 2 else 2)
        far_parts = scaled(
            jnp.concatenate([vg[f, pl.ds(0, more), :] for f in range(2)], axis=0),
            su[pl.ds(G, more), :],
            1 if k < 2 else 2,
        )
        sent = jnp.concatenate(own_parts, axis=1)
        beyond = jnp.concatenate(far_parts, axis=1)
        x, i = (x_one, k) if k < 2 else (x_two, k - 2)
        x[i, pl.ds(0, G), :] = sent

        @pl.when(ghost)
        def _():
            x[i, pl.ds(UPX, more), :] = beyond

        (faces_one if k < 2 else faces_two)[i] = faces_of(
            jnp.concatenate([sent, beyond], axis=0)
        )
        last = more - LAYER
        return [
            jnp.concatenate([a, b[:last]], axis=0) if last else a
            for a, b in zip(own_parts, far_parts)
        ]

    def gram(fields, i, j):
        product = fields[i] * fields[j]
        for f in range(2):
            part = jnp.sum(product[f * G : (f + 1) * G], axis=0, keepdims=True)
            rr[pl.ds(f * 16 + place(i, j), 1), :] = part[:, :128] + part[:, 128:]

    def gram_rows():
        sums = jnp.sum(rr[...], axis=1, keepdims=True)
        spot = iota((16, 128), 0) == iota((16, 128), 1)
        return [
            jnp.sum(jnp.where(spot, sums[f * 16 : f * 16 + 16], 0.0), axis=0, keepdims=True)
            for f in range(2)
        ]

    def start_plane(e):
        def one(i, _):
            if e == 0:
                src, dst = mp, mps.at[PLANE - 2 - i]
            elif e == 1:
                src, dst = mq, mqs.at[PLANE - 2 - i]
            else:
                src, dst = me, mes.at[PLANE - 2 - i]
            pltpu.make_async_remote_copy(
                src_ref=src, dst_ref=dst, send_sem=ps.at[e], recv_sem=pr.at[e],
                device_id=plane_peer(i), device_id_type=MESH,
            ).start()
            return 0

        lax.fori_loop(0, PLANE - 1, one, 0)

    def start_line(e):
        for o in sorted(range(1, ZLINE), key=lambda o: -min(o, ZLINE - o)):
            i = o - 1
            if e == 0:
                src, dst = mz, mzs.at[ZLINE - 2 - i]
            else:
                src, dst = tile.at[(me_z + o) % ZLINE], tiles.at[ZLINE - 2 - i]
            pltpu.make_async_remote_copy(
                src_ref=src, dst_ref=dst, send_sem=zs.at[e], recv_sem=zr.at[e],
                device_id=line_peer(i), device_id_type=MESH,
            ).start()

    def wait_all(buffer, sem):
        pltpu.make_async_copy(buffer, buffer, sem).wait()

    rr[...] = jnp.zeros(rr.shape, F32)
    sent = scaled(v[0], su[pl.ds(0, G), :], 1)

    def split3(a):
        first = a.astype(BF16).astype(F32)
        second = (a - first).astype(BF16).astype(F32)
        return [first, second, a - first - second]

    lane = iota((G, LANES), 1)
    notes = sent[0].astype(F32)
    for i, col in enumerate(kinds + split3(density)):
        notes = jnp.where(lane == DOF + i, col, notes)
    sent = jnp.concatenate([notes.astype(BF16), sent[1]], axis=1)
    x_one[0, pl.ds(0, G), :] = sent

    @pl.when(jnp.logical_not(ghost))
    def _():
        faces_one[0] = faces_of(sent)


    inner = [v[0]]
    for _ in range(ITERS - 1):
        parts = scaled(inner[-1], su[pl.ds(0, G), :], 1)
        near = jnp.concatenate(parts, axis=1)

        def empty(size):
            return jnp.zeros((size, 2 * LANES), BF16)

        moved = LOCAL_GAIN * coupled(
            [
                jnp.concatenate([empty(LAYER), near, empty(FACE_ROWS)], axis=0),
                jnp.concatenate([near, empty(LAYER + FACE_ROWS)], axis=0),
            ]
        )
        inner.append((moved + straight(parts, kinds[6])) * both(sc[pl.ds(0, G), :]))
    for i in range(ITERS):
        for j in range(i, ITERS):
            gram(inner, i, j)

    spread = iota((G, 128), 1) == iota((G, 128), 0)

    def as_row(col):
        return jnp.sum(jnp.where(spread, col, 0.0), axis=0, keepdims=True)

    rows = gram_rows()
    mp[0:1, :] = rows[0]
    mp[1:2, :] = rows[1]
    mp[2:3, :] = as_row(owners)
    mp[3:4, :] = as_row(density)

    extra = 2 * ghost.astype(jnp.int32) + behind.astype(jnp.int32)
    pl.semaphore_wait(barrier, PLANE - 1 + ZLINE - 1 + extra)

    @pl.when(ghost)
    def _():
        for m in range(2):
            far_copy(m).start()

    @pl.when(behind)
    def _():
        for m in range(2, 4):
            far_copy(m).start()

    start_halos(0, (0, 1))

    @pl.when(jnp.logical_not(ghost))
    def _():
        for d in range(2, 6):
            @pl.when(sends[d][0])
            def _():
                halo(0, d).start()

    start_plane(0)
    wait_all(mps, pr.at[0])
    mz[...] = mp[...] + total(mps[i] for i in range(PLANE - 1))
    start_line(0)

    low_half = iota((1, 128), 1) < G

    def joined(a, b):
        return jnp.where(low_half, a, pltpu.roll(b, G, 1))

    def gathered(row):
        parts = [mps[i, row : row + 1, :] for i in range(PLANE - 1)]
        parts.append(mp[row : row + 1, :])
        return [joined(parts[2 * m], parts[2 * m + 1]) for m in range(PLANE // 2)]

    q = iota((128, 1), 0)
    bins = (((q // 64 * CY + yc) * SY + gy) * SZ + q // 8 % 8) * GPB + q % 8
    bins = bins.astype(F32)
    for m, row in enumerate(gathered(2)):
        hot[:, pl.ds(m * 128, 128)] = jnp.where(row == bins, 1.0, 0.0).astype(BF16)

    masses = gathered(3)
    split[pl.ds(96, 32), :] = jnp.zeros((32, PLANE * G), BF16)

    wait_halos(0, (0, 1))

    @pl.when(ghost)
    def _():
        for m in range(4):
            far_copy(m).wait_recv()
        faces_one[0] = faces_of(x_one[0, pl.ds(0, ALL), :])
        for d in range(2, 6):
            @pl.when(sends[d][0])
            def _():
                halo(0, d, True).start()

    notes = x_one[0, pl.ds(UPX, DEEP * LAYER), pl.ds(128, 128)].astype(F32)
    notes = [notes[:, DOF - 128 + i : DOF - 127 + i] for i in range(10)]
    prepare(G, DEEP * LAYER, notes[:7], notes[7] + notes[8] + notes[9])
    kind = jnp.concatenate([kinds[6], notes[6]], axis=0)
    beyond = su[pl.ds(G, DEEP * LAYER), :]
    beyond = jnp.where(beyond > 0.0, 1.0 / beyond, 0.0)
    parts = []
    for f in range(2):
        parts.append(x_one[0, pl.ds(0, ALL), pl.ds(f * LANES, LANES)])
        vg[f] = parts[f][G:].astype(F32) * beyond

    spots = {}
    for i in range(ITERS):
        for j in range(ITERS):
            n = len(spots)
            spots[i, j] = n % 8 + 16 * (n // 8)
    for i in range(ITERS):
        spots[i, ITERS] = 8 + i
        spots[ITERS, i] = 24 + i
    lane = iota((G, 128), 1)
    columns = [jnp.zeros((G, 128), F32)]

    def products(i, j):
        part = v[i, pl.ds(G, G), :] * rp[pl.ds(0, G), :] * v[j, pl.ds(0, G), :]
        col = jnp.sum(part, axis=1, keepdims=True)
        columns[0] = jnp.where(lane == spots[i, j], col, columns[0])

    def turned(at):
        rows = jnp.transpose(jnp.concatenate([columns[0], jnp.zeros((G, 128), F32)], axis=0))
        return jnp.where(
            low_half, rows[at : at + 8], pltpu.roll(rows[at + 16 : at + 24], G, 1)
        )

    guess = None
    for k in range(ITERS):
        size = ALL - k * LAYER
        alone = straight(parts, kind[:size])
        wait_halos(k, range(2, 6) if k == 0 else range(6))
        moved = (coupled(sources_of(k, size // LAYER)) + alone) * both(sc[pl.ds(0, size), :])
        ours = jnp.concatenate([moved[:G], moved[size : size + G]], axis=0)
        if k == 0:
            wait_all(mzs, zr.at[0])
            row = mz[0:2, :] + total(mzs[i, 0:2, :] for i in range(ZLINE - 1))
            guess, _, _ = sweeps(
                entries(row, ITERS), ITERS - 1, lambda c: {i + 1: e for i, e in c.items()}
            )
            guess = [jnp.where((s > 1e-3) & (s < 1e6), s, 1.0) for s in guess]
        if k < ITERS - 1:
            step = jnp.concatenate(
                [jnp.broadcast_to(guess[k][f : f + 1], (G, 1)) for f in range(2)], axis=0
            )
            v[k + 1] = v[k] - step * ours
            for f in range(2):
                more = size - G
                vg[f, pl.ds(0, more), :] = (
                    vg[f, pl.ds(0, more), :]
                    - guess[k][f : f + 1] * moved[f * size + G : (f + 1) * size]
                )
            parts = ship(k + 1)
            start_halos(k + 1)
        else:
            v[k + 1] = ours
        for i in range(k + 2):
            gram(v, i, k + 1)
        if k == 0:
            gram(v, 0, 0)
            products(0, 0)
        for i in range(k + 1):
            products(i, k + 1)
            products(k + 1, i)
        if 0 < k + 1 < ITERS:
            products(k + 1, k + 1)
        if k == ITERS - 2:
            me[...] = turned(0)
            start_plane(2)

    rows = gram_rows()
    mq[...] = turned(8)
    mq[4:5, :] = rows[0]
    mq[5:6, :] = rows[1]
    start_plane(1)
    wait_all(mes, pr.at[2])
    wait_all(mqs, pr.at[1])
    sums = mq[4:6, :] + total(mqs[i, 4:6, :] for i in range(PLANE - 1))

    def message(i):
        parts = [mes[i], mqs[i]] if i < PLANE - 1 else [me[...], mq[...]]
        return jnp.concatenate(parts, axis=0)

    sub = iota((16, 128), 0)
    for m in range(PLANE // 2):
        a, b = message(2 * m), message(2 * m + 1)
        low = jnp.where(low_half, a, pltpu.roll(b, G, 1))
        high = jnp.where(low_half, pltpu.roll(a, G, 1), b)
        low = jnp.where(sub < 12, low, jnp.where(sub == 12, masses[m], 0.0))
        high = jnp.where(sub < 12, high, 0.0)
        for i, part in enumerate(split3(jnp.concatenate([low, high], axis=0))):
            split[pl.ds(i * 32, 32), pl.ds(m * 128, 128)] = part.astype(BF16)
    blocks = lax.dot_general(hot[...], split[...], NT_DIMS, preferred_element_type=F32)
    blocks = blocks + pltpu.roll(blocks, 96, 1) + pltpu.roll(blocks, 64, 1)
    lane = iota((8, 128), 1)
    first = iota((8, 128), 0) == 0
    shared = jnp.where(
        first & (lane >= 32) & (lane < 48),
        pltpu.roll(sums, 32, 1)[0:1],
        jnp.where(first & (lane >= 48) & (lane < 64), pltpu.roll(sums, 48, 1)[1:2], 0.0),
    )
    for i in range(ZLINE):
        full = jnp.where(lane < 32, blocks[i * 8 : (i + 1) * 8], shared)
        tile[i] = jnp.where(low_half, full[0:4], pltpu.roll(full, G, 1)[4:8])
    start_line(1)
    wait_all(tiles, zr.at[1])
    mine = tile[me_z] + total(tiles[i] for i in range(ZLINE - 1))
    mine = jnp.concatenate([mine, pltpu.roll(mine, G, 1)], axis=0)
    row = jnp.concatenate(
        [pltpu.roll(mine, 96, 1)[0:1], pltpu.roll(mine, 80, 1)[0:1]], axis=0
    )

    inverse = [1.0 / s for s in guess]

    def newton(c):
        out = {}
        for i, e in c.items():
            if i < ITERS - 1:
                part = e * inverse[i]
                out[i] = out[i] + part if i in out else part
                out[i + 1] = out[i + 1] - part if i + 1 in out else -part
            else:
                out[i + 1] = e
        return out

    _, answer, left = sweeps(entries(row, ITERS + 1), ITERS, newton)

    def combine(coefficients, f):
        return total(
            c[f : f + 1, :] * v[i, pl.ds(f * G, G), :] for i, c in coefficients.items()
        )

    solved = [combine(answer, f) * rp[pl.ds(0, G), :] for f in range(2)]
    for a in range(NX):
        for f, out in enumerate((state_out, adjoint_out)):
            out[own[a]] = solved[f][a * LAYER : (a + 1) * LAYER, :DOF].reshape(NY, NZ, DOF)
    applied = {i: (1.0 - c if i == 0 else -c) for i, c in left.items()}
    lane = iota((1, 128), 1)
    weights = jnp.zeros((1, 128), F32)
    for (i, j), spot in spots.items():
        terms = []
        if i < ITERS:
            terms.append(answer[i][1:2] * applied[j][0:1])
        if j < ITERS:
            terms.append(answer[j][0:1] * applied[i][1:2])
        weights = jnp.where(lane == spot, total(terms), weights)
    above = -1.5 * jnp.sum(mine * weights, axis=1, keepdims=True)
    below = mine[:, 12:13]
    ratio = jnp.where(below > 0.0, above / below, 0.0)
    coarse_out[...] = jnp.sum(jnp.where(eye8, ratio, 0.0), axis=0, keepdims=True)

    for k in range(ITERS):
        for_halos(k, range(6), [c for c, _ in sends], lambda copy: copy.wait_send())

    @pl.when(ghost)
    def _():
        for m in range(2):
            far_copy(m).wait_send()

    @pl.when(behind)
    def _():
        for m in range(2, 4):
            far_copy(m).wait_send()

    for buffer, sem in (
        (mps, ps.at[0]),
        (mqs, ps.at[1]),
        (mes, ps.at[2]),
        (mzs, zs.at[0]),
        (tiles, zs.at[1]),
    ):
        wait_all(buffer, sem)


def local(body_load, probe_load, density, link_types, off_blocks, self_blocks, block_owner):
    vmem = pl.BlockSpec(memory_space=pltpu.VMEM)
    state, adjoint, coarse = pl.pallas_call(
        kernel,
        out_shape=(
            pltpu.VMEM(body_load.shape, F32),
            pltpu.VMEM(body_load.shape, F32),
            pltpu.VMEM((1, GPB), F32),
        ),
        in_specs=[vmem] * 7,
        out_specs=(vmem,) * 3,
        scratch_shapes=[
            pltpu.VMEM((2, ROWS, 2 * LANES), BF16),
            pltpu.VMEM((2, ROWS, 4 * LANES), BF16),
            pltpu.VMEM((2, FACE_ROWS, 2 * LANES), BF16),
            pltpu.VMEM((2, FACE_ROWS, 4 * LANES), BF16),
            pltpu.VMEM((2, DEEP * LAYER, LANES), F32),
            pltpu.VMEM((5, 8 * LAYER, SOURCES), BF16),
            pltpu.VMEM((12 * LANES, LANES), BF16),
            pltpu.VMEM((ITERS + 1, 2 * G, LANES), F32),
            pltpu.VMEM((ALL, LANES), F32),
            pltpu.VMEM((ALL, LANES), F32),
            pltpu.VMEM((ALL, LANES), F32),
            pltpu.VMEM((128, PLANE * G), BF16),
            pltpu.VMEM((32, 128), F32),
            pltpu.VMEM((4, 128), F32),
            pltpu.VMEM((PLANE - 1, 4, 128), F32),
            pltpu.VMEM((4, 128), F32),
            pltpu.VMEM((ZLINE - 1, 4, 128), F32),
            pltpu.VMEM((8, 128), F32),
            pltpu.VMEM((PLANE - 1, 8, 128), F32),
            pltpu.VMEM((8, 128), F32),
            pltpu.VMEM((PLANE - 1, 8, 128), F32),
            pltpu.VMEM((128, PLANE * G), BF16),
            pltpu.VMEM((ZLINE, 4, 128), F32),
            pltpu.VMEM((ZLINE - 1, 4, 128), F32),
            pltpu.SemaphoreType.DMA((ITERS, 6)),
            pltpu.SemaphoreType.DMA((ITERS, 6)),
            pltpu.SemaphoreType.DMA((4,)),
            pltpu.SemaphoreType.DMA((4,)),
            pltpu.SemaphoreType.DMA((3,)),
            pltpu.SemaphoreType.DMA((3,)),
            pltpu.SemaphoreType.DMA((2,)),
            pltpu.SemaphoreType.DMA((2,)),
        ],
        compiler_params=pltpu.CompilerParams(
            collective_id=0, has_side_effects=True, vmem_limit_bytes=60 << 20
        ),
        name="sweeps",
    )(
        body_load,
        probe_load,
        density,
        jnp.transpose(link_types, (0, 3, 1, 2)),
        off_blocks,
        self_blocks,
        block_owner,
    )
    return state, adjoint, coarse.reshape(GPB)


def solution(mesh):
    in_specs = (
        P("gx", "gy", "gz", None),
        P("gx", "gy", "gz", None),
        P("gx", "gy", "gz"),
        P("gx", "gy", "gz", None),
        P(),
        P(),
        P("gx", "gy", "gz"),
    )
    out_specs = (P("gx", "gy", "gz", None), P("gx", "gy", "gz", None), P(("gx", "gy", "gz")))
    return jax.shard_map(local, mesh=mesh, in_specs=in_specs, out_specs=out_specs, check_vma=False)
```
